32 devices in a mesh: row: 4 (over y, x), col: 4 (over z), layer: 2 (over core).
Axes of the slice: x: 2, y: 2, z: 4, core: 2. Of those that a mesh axis runs over, the one named last changes fastest.
Arguments:
- earlier_warming_amount: float32 [8, 512, 512], P('layer', 'row', 'col'), may hold values from -2 to 2
- conductive_capability: float32 [8, 512, 512], P('layer', 'row', 'col'), may hold values from 0.5 to 2
- thermal_mass_timewise: float32 [8, 512, 512], P('layer', 'row', 'col'), may hold values from 0.5 to 2
- toggling_wattage_map: bfloat16 [32, 64, 4096], P(('row', 'col', 'layer')), may hold values from 0.049804688 to 1
- baseline_loss_wattage: bfloat16 [32, 64, 4096], P(('row', 'col', 'layer')), may hold values from 0.049804688 to 1
- receiving_panel: int32 [32, 64, 1], P(('row', 'col', 'layer')), may hold values from 0 to 15; in each aligned block of 64 rows (0 to 63, 64 to 127, ..., all dimensions but the last counted through in order) at most 4 rows name the same one
- subsquare_placement: int32 [32, 64], P(('row', 'col', 'layer')), may hold values from 0 to 3
- holder_chip_module: int32 [32, 64], P(('row', 'col', 'layer')), may hold values from 0 to 15, never falling along the last dimension, each value on 1 to 8 neighbouring positions
- module_tier_order: int32 [32, 16], P(('row', 'col', 'layer')), may hold values from 0 to 3
- warming_sensitivity: float32 [32, 16], P(('row', 'col', 'layer')), may hold values from 0.5 to 2
Outputs:
- new_temperature: float32 [8, 512, 512], P('layer', 'row', 'col')
- supplied_wattage_density: float32 [8, 512, 512], P('layer', 'row', 'col')
The draws below stay inside these ranges and needn't reach their ends.
Inputs may be any that keep to these rules, and one draw needn't show every extreme that they name: `receiving_panel`: the tile is numbered row tile times the number of column tiles plus column tile, inside the owning device's layer group; among the slots of one device at most 4 name the same tile, and exactly 4 do on some device in every draw. `subsquare_placement`: row-major over the tile's patch rows and patch columns. `holder_chip_module`: never falls along a device's slots; every block of a device has 1 to 8 slots.
All inputs are finite; a program needn't handle non-finite values.
Results may differ from the reference program's by a relative error of at most 0.0012.
Values may be sent and summed in bfloat16 or wider, within the bound.
A program may use at most 64 MiB of HBM per device.

```python
import math
import jax
import jax.numpy as jnp
import numpy as np
from jax import lax

SUBSQUARE_EXTENT = 64
CR = 128
CC = 128
CL = 4
SWEEPS = 3
S = 64
NB_DEV = 16
CAP = 4
NLAY = 8
NROWS = 512
NCOLS = 512
N_ROW = 4
N_COL = 4
N_LAYER = 2
DEVICES = 32


def draw_earlier_warming_amount(key, part):
    first_key, second_key = jax.random.split(jax.random.fold_in(key, 11))
    coarse_shape = (NLAY, NROWS // SUBSQUARE_EXTENT, NCOLS // SUBSQUARE_EXTENT)
    coarse = jax.random.uniform(first_key, coarse_shape, jnp.float32, -1.0, 1.0)
    fine = 0.3 * jnp.clip(jax.random.normal(second_key, (NLAY, NROWS, NCOLS), jnp.float32), -3.0, 3.0)
    spread_out = jnp.repeat(jnp.repeat(coarse, SUBSQUARE_EXTENT, axis=1), SUBSQUARE_EXTENT, axis=2)
    return spread_out + fine


def touch_ends(values, key, least, top_value):
    shape = values.shape
    place = [jax.random.randint(jax.random.fold_in(key, axis), (), 0, shape[axis]) for axis in range(len(shape))]
    values = values.at[tuple(place)].set(least)
    longest = shape.index(max(shape))
    place[longest] = (place[longest] + 1) % shape[longest]
    return values.at[tuple(place)].set(top_value)


def level_of(rng, shape, cuts, low, high):
    gain = 1.0
    for position, blocks in cuts:
        draws = jax.random.uniform(jax.random.fold_in(jax.random.fold_in(rng, 6), position), (blocks,), jnp.float32, low / len(cuts), high / len(cuts))
        gain = gain * jnp.repeat(jnp.exp(draws), shape[position] // blocks).reshape((-1,) + (1,) * (len(shape) - 1 - position))
    return gain


def split_up(count, total, reach, lean):
    loads = [(1 << 20) // math.isqrt(rank ** lean) + 1 for rank in range(2, count + 1)]
    rest, holding = total - reach - (count - 1), [1] * (count - 1)
    while rest > 0:
        free = [i for i in range(count - 1) if holding[i] < reach]
        mass, budget = sum([loads[i] for i in free]), rest
        for i in free:
            more = min(reach - holding[i], max(1, budget * loads[i] // mass), rest)
            holding[i] = holding[i] + more
            rest = rest - more
    return np.array([reach] + holding)


def ragged_sizes(stream_key, number_of, total, bound, slope):
    if number_of == 2:
        one = jax.random.randint(stream_key, (), max(1, total - bound), min(bound, total - 1) + 1)
        return jnp.stack([one, total - one])
    sizes = jnp.asarray(split_up(number_of, total, bound, slope), jnp.int32)
    pairs = (number_of - 1) // 2
    source_of, taker = sizes[1:1 + 2 * pairs:2], sizes[2:2 + 2 * pairs:2]
    margin = jnp.minimum(source_of - 1, bound - taker)
    shifted = jax.random.randint(jax.random.fold_in(stream_key, 1), (pairs,), 0, 1 << 20) % (margin + 1)
    sizes = sizes.at[1:1 + 2 * pairs:2].set(source_of - shifted).at[2:2 + 2 * pairs:2].set(taker + shifted)
    return sizes[jax.random.permutation(jax.random.fold_in(stream_key, 2), number_of)]


def routed_block(stream_key, own, number, rows, count, top, reach, skew):
    sequence = jax.random.permutation(stream_key, count)
    crowded, common = load_shares(count, rows * top, reach, skew, True), load_shares(count, rows * top, reach, skew, False)
    places = jnp.arange(count)

    def named(lengths, turn):
        used = int((lengths > 0).sum())
        fixed = max(1, used // 4)
        passed = fixed + (places - fixed + turn * (used - fixed)) % max(1, count - fixed)
        return jnp.zeros((count,), jnp.int32).at[sequence[jnp.where(places < fixed, places, passed)]].set(jnp.asarray(lengths, jnp.int32))

    lengths = jnp.where(number % 4 == 0, named(crowded, number // 4), named(common, number - number // 4 - 1))
    mixed = jax.random.permutation(jax.random.fold_in(own, 3), count)
    donor, taker = mixed[0:count // 2 * 2:2], mixed[1:count // 2 * 2:2]
    room = jnp.minimum(lengths[donor] - 1, reach - lengths[taker]) // 2
    room = jnp.where((donor == sequence[0]) | (taker == sequence[0]) | (lengths[taker] == 0), 0, jnp.maximum(room, 0))
    passed = jax.random.randint(jax.random.fold_in(own, 4), (count // 2,), 0, 1 << 20) % (room + 1)
    lengths = lengths.at[donor].add(-passed).at[taker].add(passed)
    members = jnp.searchsorted(jnp.cumsum(lengths), jnp.arange(rows * top), side="right").astype(jnp.int32)
    listing = members.reshape(top, rows).T
    listing = listing[jax.random.permutation(jax.random.fold_in(own, 1), rows)]
    turn = jax.random.randint(jax.random.fold_in(own, 2), (rows, 1), 0, top)
    return jnp.take_along_axis(listing, (jnp.arange(top)[None, :] + turn) % top, axis=1)


def load_shares(amount, total, most, skew, full):
    loads = [(1 << 20) // math.isqrt(rank ** skew) + 1 for rank in range(1, amount + 1)]
    largest = most if full else min(most, max(-(-total // amount), total * loads[0] // sum(loads)))
    least = 1 if total - largest >= amount - 1 else 0
    holding, rest = [largest] + [least] * (amount - 1), total - largest - least * (amount - 1)
    while rest > 0:
        free = [i for i in range(1, amount) if holding[i] < largest] or [i for i in range(1, amount) if holding[i] < most]
        whole, remaining = sum([loads[i] for i in free]), rest
        for i in free:
            more = min(most - holding[i], max(1, remaining * loads[i] // whole), rest)
            holding[i] = holding[i] + more
            rest = rest - more
    return np.array(holding)


def setup_inputs(seed: int = 0) -> dict:
    keys = jax.random.split(jax.random.key(seed), 11)
    earlier_warming_amount = draw_earlier_warming_amount(jax.random.fold_in(keys[10], 71), 0)
    conductive_capability = jnp.clip(jnp.exp(math.log(2.0) - 1.3862944 * jax.random.uniform(keys[1], (NLAY, NROWS, NCOLS), jnp.float32) ** level_of(keys[1], (NLAY, NROWS, NCOLS), ((0, 2), (1, 4), (2, 4)), -0.2, 0.2)), 0.5, 2.0)
    thermal_mass_timewise = jnp.clip(0.5 + 1.5 * jax.random.uniform(keys[2], (NLAY, NROWS, NCOLS), jnp.float32) ** level_of(keys[2], (NLAY, NROWS, NCOLS), ((0, 2), (1, 4), (2, 4)), -0.2, 0.2), 0.5, 2.0)
    toggling_wattage_map = jnp.clip(jnp.exp(math.log(1.0) - 2.9996462 * jax.random.uniform(keys[3], (DEVICES, S, SUBSQUARE_EXTENT * SUBSQUARE_EXTENT), jnp.float32) ** level_of(keys[3], (DEVICES, S, SUBSQUARE_EXTENT * SUBSQUARE_EXTENT), ((0, 32),), -0.2, 0.2)), 0.049804688, 1.0).astype(jnp.bfloat16)
    baseline_loss_wattage = jnp.clip(jnp.exp(math.log(1.0) - 2.9996462 * jax.random.uniform(keys[4], (DEVICES, S, SUBSQUARE_EXTENT * SUBSQUARE_EXTENT), jnp.float32) ** level_of(keys[4], (DEVICES, S, SUBSQUARE_EXTENT * SUBSQUARE_EXTENT), ((0, 32),), -0.2, 0.2)), 0.049804688, 1.0).astype(jnp.bfloat16)
    receiving_panel_keys = jax.random.split(jax.random.fold_in(keys[5], 1), DEVICES * S // S)
    receiving_panel_turns = jax.random.permutation(jax.random.fold_in(keys[5], 3), DEVICES * S // S)
    receiving_panel = jax.vmap(lambda own, number: routed_block(jax.random.fold_in(keys[5], 2), own, number, S, N_ROW * N_COL, 1, CAP, 2))(receiving_panel_keys, receiving_panel_turns).reshape((DEVICES, S, 1))
    subsquare_placement = touch_ends(jax.random.randint(keys[6], (DEVICES, S), 0, (CR // SUBSQUARE_EXTENT) * (CC // SUBSQUARE_EXTENT)), jax.random.fold_in(keys[6], 1), 0, ((CR // SUBSQUARE_EXTENT) * (CC // SUBSQUARE_EXTENT)) - 1).astype(jnp.int32)
    holder_chip_module = jax.vmap(lambda own: jnp.searchsorted(jnp.cumsum(ragged_sizes(own, NB_DEV, S, 2 * S // NB_DEV, 2)), jnp.arange(S), side="right"))(jax.random.split(keys[7], DEVICES)).reshape((DEVICES, S)).astype(jnp.int32)
    module_tier_order = touch_ends(jax.random.randint(keys[8], (DEVICES, NB_DEV), 0, CL), jax.random.fold_in(keys[8], 1), 0, CL - 1).astype(jnp.int32)
    warming_sensitivity = jnp.clip(jnp.exp(math.log(2.0) - 1.3862944 * jax.random.uniform(keys[9], (DEVICES, NB_DEV), jnp.float32) ** level_of(keys[9], (DEVICES, NB_DEV), ((0, 32),), -0.2, 0.2)), 0.5, 2.0)
    return dict(earlier_warming_amount=earlier_warming_amount, conductive_capability=conductive_capability, thermal_mass_timewise=thermal_mass_timewise, toggling_wattage_map=toggling_wattage_map, baseline_loss_wattage=baseline_loss_wattage, receiving_panel=receiving_panel, subsquare_placement=subsquare_placement, holder_chip_module=holder_chip_module, module_tier_order=module_tier_order, warming_sensitivity=warming_sensitivity)


eig_low = 0.1
eig_high = 2.0


def neighbours(padded):
    return [padded[2:, 1:-1, 1:-1], padded[:-2, 1:-1, 1:-1], padded[1:-1, 2:, 1:-1],
            padded[1:-1, :-2, 1:-1], padded[1:-1, 1:-1, 2:], padded[1:-1, 1:-1, :-2]]


def face_terms(padded_cond):
    center = padded_cond[1:-1, 1:-1, 1:-1]
    return [0.5 * (center + beside) for beside in neighbours(padded_cond)]


def diagonal_of(thermal_mass_timewise, nearby_conductance_factors):
    running = thermal_mass_timewise
    for face_term in nearby_conductance_factors:
        running = running + face_term
    return running


def linear_mapping_result(padded, nearby_conductance_factors, linear_pivot_coefficients):
    result = linear_pivot_coefficients * padded[1:-1, 1:-1, 1:-1]
    for face_term, beside in zip(nearby_conductance_factors, neighbours(padded)):
        result = result - face_term * beside
    return result


def reference(earlier_warming_amount, conductive_capability, thermal_mass_timewise, toggling_wattage_map, baseline_loss_wattage, receiving_panel, subsquare_placement, holder_chip_module, module_tier_order, warming_sensitivity):
    third_axis_extent, first_axis_extent, second_axis_extent = earlier_warming_amount.shape
    subsquares_eastward = first_axis_extent // SUBSQUARE_EXTENT
    subsquares_northward = second_axis_extent // SUBSQUARE_EXTENT
    slots_all = DEVICES * S
    owner = jnp.arange(slots_all, dtype=jnp.int32) // S
    owner_group = owner % N_LAYER
    target = receiving_panel.reshape(slots_all).astype(jnp.int32)
    local_block = holder_chip_module.reshape(slots_all).astype(jnp.int32)
    global_block = owner * NB_DEV + local_block
    die_layer = module_tier_order.reshape(DEVICES * NB_DEV)[global_block] + owner_group * CL
    offsets = subsquare_placement.reshape(slots_all)
    patch_row = (target // N_COL) * (CR // SUBSQUARE_EXTENT) + offsets // (CC // SUBSQUARE_EXTENT)
    patch_col = (target % N_COL) * (CC // SUBSQUARE_EXTENT) + offsets % (CC // SUBSQUARE_EXTENT)
    patch_index = ((die_layer * subsquares_eastward + patch_row) * subsquares_northward + patch_col).astype(jnp.int32)
    subsquare_averaged = earlier_warming_amount.reshape(third_axis_extent, subsquares_eastward, SUBSQUARE_EXTENT, subsquares_northward, SUBSQUARE_EXTENT).mean(axis=(2, 4)).reshape(-1)
    slot_means = subsquare_averaged[patch_index]
    blocks_all = DEVICES * NB_DEV
    block_sums = jax.ops.segment_sum(slot_means, global_block, num_segments=blocks_all)
    block_sizes = jax.ops.segment_sum(jnp.ones((slots_all,), jnp.float32), global_block, num_segments=blocks_all)
    factor = jnp.exp(warming_sensitivity.reshape(blocks_all) * (block_sums / block_sizes))
    slot_power = toggling_wattage_map.reshape(slots_all, SUBSQUARE_EXTENT * SUBSQUARE_EXTENT).astype(jnp.float32) + factor[global_block][:, None] * baseline_loss_wattage.reshape(slots_all, SUBSQUARE_EXTENT * SUBSQUARE_EXTENT).astype(jnp.float32)
    slot_power = lax.optimization_barrier(slot_power.astype(jnp.bfloat16)).astype(jnp.float32)
    footprint_wattage = jax.ops.segment_sum(slot_power, patch_index, num_segments=third_axis_extent * subsquares_eastward * subsquares_northward)
    supplied_wattage_density = footprint_wattage.reshape(third_axis_extent, subsquares_eastward, subsquares_northward, SUBSQUARE_EXTENT, SUBSQUARE_EXTENT).transpose(0, 1, 3, 2, 4).reshape(third_axis_extent, first_axis_extent, second_axis_extent)
    nearby_conductance_factors = face_terms(jnp.pad(conductive_capability, 1))
    linear_pivot_coefficients = diagonal_of(thermal_mass_timewise, nearby_conductance_factors)
    middle = (eig_low + eig_high) / 2.0
    spread = (eig_high - eig_low) / 2.0
    ratio_sigma = middle / spread
    weight_now = 1.0 / ratio_sigma
    iterate_guess = earlier_warming_amount
    remaining_imbalance = thermal_mass_timewise * earlier_warming_amount + supplied_wattage_density - linear_mapping_result(jnp.pad(iterate_guess, 1), nearby_conductance_factors, linear_pivot_coefficients)
    direction = remaining_imbalance / (linear_pivot_coefficients * middle)
    for sweep in range(SWEEPS):
        iterate_guess = iterate_guess + direction
        if sweep < SWEEPS - 1:
            remaining_imbalance = remaining_imbalance - linear_mapping_result(jnp.pad(direction, 1), nearby_conductance_factors, linear_pivot_coefficients)
            weight_new = 1.0 / (2.0 * ratio_sigma - weight_now)
            direction = weight_new * weight_now * direction + (2.0 * weight_new / spread) * (remaining_imbalance / linear_pivot_coefficients)
            weight_now = weight_new
    return iterate_guess, supplied_wattage_density
```

```python
import functools
import jax
import jax.numpy as jnp
from jax import lax
from jax.experimental import pallas as pl
from jax.experimental.pallas import tpu as pltpu
from jax.sharding import PartitionSpec as P

SUB = 64
SWEEPS = 3
CAP = 4
EIG_LOW = 0.1
EIG_HIGH = 2.0
LANES = 128
PACK = 16

MESH = pl.DeviceIdType.MESH
F32 = jnp.float32
BF16 = jnp.bfloat16


def iota(shape, dim):
    return lax.broadcasted_iota(jnp.int32, shape, dim)


def hi_dot(a, b, dims):
    return lax.dot_general(
        a, b, (dims, ((), ())), precision=lax.Precision.HIGHEST, preferred_element_type=F32
    )


def kernel(
    sizes,
    temp_hbm,
    cond_hbm,
    mass_hbm,
    dyn_hbm,
    leak_hbm,
    panel_ref,
    place_ref,
    block_ref,
    tier_ref,
    sens_ref,
    out_ref,
    power_ref,
    temp,
    cond,
    mass,
    dyn,
    leak,
    note_send,
    note_recv,
    load_send,
    load_recv,
    dirs,
    faces,
    diag,
    inv,
    resid,
    edge_send,
    edge_recv,
    plane_recv,
    in_sem,
    note_ssem,
    note_rsem,
    load_ssem,
    load_rsem,
    halo_ssem,
    halo_rsem,
):
    n_row, n_col, n_layer = sizes
    tiles = n_row * n_col
    tiers, rows, cols = temp.shape
    slots, cells = dyn.shape
    folds = PACK // CAP
    wide = cells // folds
    note_rows = note_send.shape[0] // tiles
    in_plane = (rows // SUB) * (cols // SUB)
    patches = tiers * in_plane
    bands = tiers * (rows // SUB)
    chunks = tiles * PACK // LANES

    my_row = lax.axis_index("row")
    my_col = lax.axis_index("col")
    my_layer = lax.axis_index("layer")
    me = my_row * n_col + my_col

    loads = [
        pltpu.make_async_copy(src, dst, in_sem.at[i])
        for i, (src, dst) in enumerate(
            (
                (temp_hbm, temp),
                (cond_hbm, cond),
                (dyn_hbm.at[0], dyn),
                (leak_hbm.at[0], leak),
                (mass_hbm, mass),
            )
        )
    ]
    for load in loads:
        load.start()

    def peer(step):
        other = lax.rem(me + step, tiles)
        return other, {"row": other // n_col, "col": lax.rem(other, n_col)}

    sides = (
        (my_layer > 0, {"layer": my_layer - 1}, 0),
        (my_layer < n_layer - 1, {"layer": my_layer + 1}, 1),
        (my_row > 0, {"row": my_row - 1}, 2),
        (my_row < n_row - 1, {"row": my_row + 1}, 3),
        (my_col > 0, {"col": my_col - 1}, 4),
        (my_col < n_col - 1, {"col": my_col + 1}, 5),
    )

    barrier = pltpu.get_barrier_semaphore()

    @pl.loop(1, tiles)
    def _(step):
        _, where = peer(step)
        pl.semaphore_signal(barrier, inc=1, device_id=where, device_id_type=MESH)

    for exists, where, side in sides[:2]:

        @pl.when(exists)
        def _(where=where):
            pl.semaphore_signal(barrier, inc=1, device_id=where, device_id_type=MESH)

    for turn in range(4):
        for exists, _, side in sides:

            @pl.when(jnp.logical_not(exists))
            def _(turn=turn, side=side):
                if side < 2:
                    plane_recv[turn, side] = jnp.zeros((rows, cols), F32)
                else:
                    edge_recv[turn, side - 2] = jnp.zeros(edge_recv.shape[2:], F32)

    lane_s = iota((slots, slots), 1)
    sub_s = iota((slots, slots), 0)
    eye = lane_s == sub_s

    def to_col(row):
        return jnp.sum(jnp.where(eye, jnp.broadcast_to(row, (slots, slots)), 0.0), axis=1, keepdims=True)

    def to_row(col):
        return jnp.sum(jnp.where(eye, jnp.broadcast_to(col, (slots, slots)), 0.0), axis=0, keepdims=True)

    tgt_col = panel_ref[...].astype(F32)
    tgt_row = to_row(tgt_col)
    blk_row = block_ref[...].astype(F32)
    blk_col = to_col(blk_row)
    sub_col = to_col(place_ref[...].astype(F32))
    same_tile = tgt_col == tgt_row
    rank_col = jnp.sum(jnp.where(same_tile & (lane_s < sub_s), 1.0, 0.0), axis=1, keepdims=True)
    rank_row = jnp.sum(jnp.where(same_tile & (sub_s < lane_s), 1.0, 0.0), axis=0, keepdims=True)
    blocks = tier_ref.shape[1]
    of_block = blk_col == iota((slots, blocks), 1).astype(F32)
    tier_col = jnp.sum(jnp.where(of_block, tier_ref[...].astype(F32), 0.0), axis=1, keepdims=True)
    sens_col = jnp.sum(jnp.where(of_block, sens_ref[...], 0.0), axis=1, keepdims=True)
    pos_col = tier_col * in_plane + sub_col
    same_block = jnp.where(blk_col == blk_row, 1.0, 0.0)
    block_size = jnp.sum(same_block, axis=1, keepdims=True)

    offset = lax.rem(me * PACK, LANES)
    my_chunk = (me * PACK) // LANES
    rel = iota((slots, LANES), 1) - offset
    fits = (rel >= 0) & (rel < PACK) & ((rel & (CAP - 1)).astype(F32) == rank_col)
    place_lanes = jnp.where(fits, pos_col + 1.0, 0.0)
    note_i = iota((tiles * note_rows, slots), 0)
    to_tile = jnp.where(
        ((note_i // note_rows).astype(F32) == tgt_row) & (lax.rem(note_i, note_rows) == 1 + my_chunk),
        1.0,
        0.0,
    )
    places = jnp.dot(to_tile.astype(BF16), place_lanes.astype(BF16), preferred_element_type=F32)

    loads[0].wait()
    band_sums = jnp.concatenate(
        [
            jnp.sum(temp[t, b * SUB : (b + 1) * SUB, :], axis=0, keepdims=True)
            for t in range(tiers)
            for b in range(rows // SUB)
        ],
        axis=0,
    )
    lane_b = iota((bands, LANES), 1)
    sub_b = iota((bands, LANES), 0)
    means = jnp.zeros((1, LANES), F32)
    per_band = cols // SUB
    for part in range(per_band):
        total = jnp.sum(jnp.where(lane_b // SUB == part, band_sums, 0.0), axis=1, keepdims=True)
        means = means + jnp.sum(
            jnp.where(lane_b == sub_b * per_band + part, total, 0.0), axis=0, keepdims=True
        )
    means = means * (1.0 / (SUB * SUB))
    note_j = iota((tiles * note_rows, LANES), 0)
    note_send[...] = places + jnp.where(lax.rem(note_j, note_rows) == 0, means, 0.0)

    sub8 = iota((2 * tiers, LANES), 0)
    lane8 = iota((2 * tiers, LANES), 1)

    def halo_copy(turn, field, where, side, lands):
        if side < 2:
            src = field.at[0 if side == 0 else tiers - 1]
            dst = plane_recv.at[turn, lands]
        else:
            src = edge_send.at[turn, (side - 2) // 2]
            dst = edge_recv.at[turn, lands - 2]
        return pltpu.make_async_remote_copy(
            src_ref=src,
            dst_ref=dst,
            send_sem=halo_ssem.at[turn, side],
            recv_sem=halo_rsem.at[turn, lands],
            device_id=where,
            device_id_type=MESH,
        )

    def pack_edges(turn, field):
        for end in range(2):
            at = end * (rows - 1)
            for t in range(tiers):
                edge_send[turn, 0, end * tiers + t : end * tiers + t + 1, :] = field[t, at : at + 1, :]
        columns = jnp.zeros((2 * tiers, rows), F32)
        for t in range(tiers):
            pick = jnp.where(
                ((sub8 == t) & (lane8 == 0)) | ((sub8 == tiers + t) & (lane8 == cols - 1)), 1.0, 0.0
            )
            columns = columns + hi_dot(pick, field[t], ((1,), (1,)))
        edge_send[turn, 1] = columns

    def each_side(act):
        for exists, where, side in sides:
            pl.when(exists)(functools.partial(act, where, side))

    def start_halo(turn, field):
        each_side(lambda where, side: halo_copy(turn, field, where, side, side ^ 1).start())

    def wait_halo(turn, field):
        each_side(lambda where, side: halo_copy(turn, field, where, side, side).wait_recv())

    def end_halo(turn, field):
        each_side(lambda where, side: halo_copy(turn, field, where, side, side ^ 1).wait_send())

    row_i = iota((rows, cols), 0)
    col_i = iota((rows, cols), 1)

    def beside(turn, field):
        ends = jnp.concatenate([edge_recv[turn, 2], edge_recv[turn, 3]], axis=0)
        sub16 = iota((4 * tiers, LANES), 0)
        lane16 = iota((4 * tiers, LANES), 1)
        result = []
        for t in range(tiers):
            v = field[t]
            low = plane_recv[turn, 0] if t == 0 else field[t - 1]
            high = plane_recv[turn, 1] if t == tiers - 1 else field[t + 1]
            north = jnp.where(
                row_i == 0, edge_recv[turn, 0, tiers + t : tiers + t + 1, :], pltpu.roll(v, 1, 0)
            )
            south = jnp.where(
                row_i == rows - 1, edge_recv[turn, 1, t : t + 1, :], pltpu.roll(v, rows - 1, 0)
            )
            put = jnp.where(
                ((sub16 == tiers + t) & (lane16 == 0))
                | ((sub16 == 2 * tiers + t) & (lane16 == cols - 1)),
                1.0,
                0.0,
            )
            rim = hi_dot(ends, put, ((0,), (0,)))
            west = jnp.where(col_i == 0, rim, pltpu.roll(v, 1, 1))
            east = jnp.where(col_i == cols - 1, rim, pltpu.roll(v, cols - 1, 1))
            result.append((v, (low, high, north, south, west, east)))
        return result

    beyond = (my_layer > 0).astype(jnp.int32) + (my_layer < n_layer - 1).astype(jnp.int32)
    pl.semaphore_wait(barrier, tiles - 1 + beyond)

    def note_copy(step):
        other, where = peer(step)
        return pltpu.make_async_remote_copy(
            src_ref=note_send.at[pl.ds(other * note_rows, note_rows), :],
            dst_ref=note_recv.at[pl.ds(me * note_rows, note_rows), :],
            send_sem=note_ssem.at[step],
            recv_sem=note_rsem.at[step],
            device_id=where,
            device_id_type=MESH,
        )

    def load_copy(step):
        other, where = peer(step)
        return pltpu.make_async_remote_copy(
            src_ref=load_send.at[pl.ds(other * PACK, PACK), :],
            dst_ref=load_recv.at[pl.ds(me * PACK, PACK), :],
            send_sem=load_ssem.at[step],
            recv_sem=load_rsem.at[step],
            device_id=where,
            device_id_type=MESH,
        )

    @pl.loop(1, tiles)
    def _(step):
        note_copy(step).start()

    own_note = pl.ds(pl.multiple_of(me * note_rows, note_rows), note_rows)
    own_copy = pltpu.make_async_copy(note_send.at[own_note, :], note_recv.at[own_note, :], note_rsem.at[0])
    own_copy.start()

    loads[1].wait()
    pack_edges(0, temp)
    start_halo(0, temp)
    pack_edges(1, cond)
    start_halo(1, cond)
    loads[2].wait()
    loads[3].wait()
    own_copy.wait()

    @pl.loop(1, tiles)
    def _(step):
        note_copy(step).wait_recv()

    note_k = iota((slots, tiles * note_rows), 1)
    from_tile = jnp.where(
        ((note_k // note_rows).astype(F32) == tgt_col) & (lax.rem(note_k, note_rows) == 0), 1.0, 0.0
    )
    tile_means = hi_dot(from_tile, note_recv[...], ((1,), (0,)))
    slot_mean = jnp.sum(
        jnp.where(iota((slots, LANES), 1).astype(F32) == pos_col, tile_means, 0.0), axis=1, keepdims=True
    )
    block_rise = jnp.sum(same_block * to_row(slot_mean), axis=1, keepdims=True) / block_size
    factor = jnp.exp(sens_col * block_rise)
    send_i = iota((tiles * PACK, slots), 0)
    goes = (
        (send_i // PACK) * CAP + lax.rem(send_i, CAP)
    ).astype(F32) == tgt_row * CAP + rank_row
    fold_i = lax.rem(send_i, PACK) // CAP
    gathered = jnp.zeros((tiles * PACK, wide), F32)
    for fold in range(folds):
        part = slice(fold * wide, (fold + 1) * wide)
        slot_power = (dyn[:, part].astype(F32) + factor * leak[:, part].astype(F32)).astype(BF16)
        pick = jnp.where(goes & (fold_i == fold), 1.0, 0.0).astype(BF16)
        gathered = gathered + jnp.dot(pick, slot_power, preferred_element_type=F32)
    load_send[...] = gathered.astype(BF16)

    @pl.loop(1, tiles)
    def _(step):
        load_copy(step).start()

    own_load = pl.ds(pl.multiple_of(me * PACK, PACK), PACK)
    own_move = pltpu.make_async_copy(load_send.at[own_load, :], load_recv.at[own_load, :], load_rsem.at[0])
    own_move.start()

    loads[4].wait()
    wait_halo(0, temp)
    wait_halo(1, cond)
    near = beside(1, cond)
    for t in range(tiers):
        c, around = near[t]
        total = mass[t]
        for k in range(6):
            face = 0.5 * (c + around[k])
            faces[k, t] = face
            total = total + face
        diag[t] = total
        inv[t] = 1.0 / total
    near = beside(0, temp)
    for t in range(tiers):
        v, around = near[t]
        value = diag[t] * v
        for k in range(6):
            value = value - faces[k, t] * around[k]
        resid[t] = mass[t] * v - value

    middle = (EIG_LOW + EIG_HIGH) / 2.0
    spread = (EIG_HIGH - EIG_LOW) / 2.0
    ratio = middle / spread
    weight = 1.0 / ratio

    sel_i = iota((folds * patches, LANES), 0)
    sel_j = iota((folds * patches, LANES), 1)
    sel_fold = sel_i // patches
    sel_in = lax.rem(sel_i, patches)
    sel_patch = lax.rem(sel_in, bands) * per_band + sel_in // bands
    fold_hit = sel_fold == lax.rem(sel_j, PACK) // CAP
    notes = note_recv[...]
    pickers = []
    for chunk in range(chunks):
        code = jnp.sum(jnp.where(lax.rem(note_j, note_rows) == 1 + chunk, notes, 0.0), axis=0, keepdims=True)
        pickers.append(
            jnp.where(fold_hit & (code == (sel_patch + 1).astype(F32)), 1.0, 0.0).astype(BF16)
        )

    own_move.wait()

    @pl.loop(1, tiles)
    def _(step):
        load_copy(step).wait_recv()

    footprint = jnp.zeros((folds * patches, wide), F32)
    for chunk in range(chunks):
        footprint = footprint + jnp.dot(
            pickers[chunk], load_recv[chunk * LANES : (chunk + 1) * LANES, :], preferred_element_type=F32
        )
    left = iota((bands, LANES), 1) < SUB
    for fold in range(folds):
        for k in range(wide // LANES):
            lanes = slice(k * LANES, (k + 1) * LANES)
            a = footprint[fold * patches : fold * patches + bands, lanes]
            b = footprint[fold * patches + bands : fold * patches + 2 * bands, lanes]
            at = 2 * (fold * (wide // LANES) + k)
            power_ref[pl.ds(at, bands, stride=SUB), :] = jnp.where(left, a, pltpu.roll(b, SUB, 1))
            power_ref[pl.ds(at + 1, bands, stride=SUB), :] = jnp.where(left, pltpu.roll(a, SUB, 1), b)

    for t in range(tiers):
        r = resid[t] + power_ref[t * rows : (t + 1) * rows, :]
        resid[t] = r
        dirs[0, t] = r * inv[t] * (1.0 / middle)
    for sweep in range(1, SWEEPS):
        field = dirs.at[sweep - 1]
        turn = 1 + sweep
        pack_edges(turn, field)
        start_halo(turn, field)
        for t in range(tiers):
            base = temp[t] if sweep == 1 else out_ref[t]
            out_ref[t] = base + field[t]
        wait_halo(turn, field)
        weight_new = 1.0 / (2.0 * ratio - weight)
        near = beside(turn, field)
        for t in range(tiers):
            v, around = near[t]
            value = diag[t] * v
            for k in range(6):
                value = value - faces[k, t] * around[k]
            r = resid[t] - value
            if sweep < SWEEPS - 1:
                resid[t] = r
            d = weight_new * weight * v + (2.0 * weight_new / spread) * (r * inv[t])
            if sweep < SWEEPS - 1:
                dirs[sweep, t] = d
            else:
                out_ref[t] = out_ref[t] + d
        weight = weight_new

    end_halo(0, temp)
    end_halo(1, cond)
    for sweep in range(1, SWEEPS):
        end_halo(1 + sweep, dirs.at[sweep - 1])

    @pl.loop(1, tiles)
    def _(step):
        note_copy(step).wait_send()
        load_copy(step).wait_send()


def shards(sizes, temp, cond, mass, dyn, leak, panel, place, block, tier, sens):
    tiers, rows, cols = temp.shape
    slots, cells = dyn.shape[1:]
    tiles = sizes[0] * sizes[1]
    folds = PACK // CAP
    note_rows = -(-(1 + tiles * PACK // LANES) // 8) * 8
    any_spec = pl.BlockSpec(memory_space=pl.ANY)
    vmem = pl.BlockSpec(memory_space=pltpu.VMEM)
    grid = (tiers, rows, cols)
    dma = pltpu.SemaphoreType.DMA
    new, power = pl.pallas_call(
        functools.partial(kernel, sizes),
        out_shape=(
            jax.ShapeDtypeStruct(grid, F32),
            jax.ShapeDtypeStruct((tiers * rows, cols), F32),
        ),
        in_specs=[any_spec] * 5 + [vmem] * 5,
        out_specs=(vmem, vmem),
        scratch_shapes=[
            pltpu.VMEM(grid, F32),
            pltpu.VMEM(grid, F32),
            pltpu.VMEM(grid, F32),
            pltpu.VMEM((slots, cells), BF16),
            pltpu.VMEM((slots, cells), BF16),
            pltpu.VMEM((tiles * note_rows, LANES), F32),
            pltpu.VMEM((tiles * note_rows, LANES), F32),
            pltpu.VMEM((tiles * PACK, cells // folds), BF16),
            pltpu.VMEM((tiles * PACK, cells // folds), BF16),
            pltpu.VMEM((SWEEPS - 1,) + grid, F32),
            pltpu.VMEM((6,) + grid, F32),
            pltpu.VMEM(grid, F32),
            pltpu.VMEM(grid, F32),
            pltpu.VMEM(grid, F32),
            pltpu.VMEM((SWEEPS + 1, 2, 2 * tiers, cols), F32),
            pltpu.VMEM((SWEEPS + 1, 4, 2 * tiers, cols), F32),
            pltpu.VMEM((SWEEPS + 1, 2, rows, cols), F32),
            dma((5,)),
            dma((tiles,)),
            dma((tiles,)),
            dma((tiles,)),
            dma((tiles,)),
            dma((SWEEPS + 1, 6)),
            dma((SWEEPS + 1, 6)),
        ],
        compiler_params=pltpu.CompilerParams(
            collective_id=0, has_side_effects=True, vmem_limit_bytes=48 * 1024 * 1024
        ),
    )(temp, cond, mass, dyn, leak, panel[0], place, block, tier, sens)
    return new, power.reshape(grid)


def solution(mesh):
    sizes = (mesh.shape["row"], mesh.shape["col"], mesh.shape["layer"])
    owner = ("row", "col", "layer")
    return jax.shard_map(
        functools.partial(shards, sizes),
        mesh=mesh,
        in_specs=(P("layer", "row", "col"),) * 3
        + (P(owner, None, None),) * 3
        + (P(owner, None),) * 4,
        out_specs=(P("layer", "row", "col"), P("layer", "row", "col")),
        check_vma=False,
    )
```

```python
import functools
import jax
import jax.numpy as jnp
from jax import lax
from jax.experimental import pallas as pl
from jax.experimental.pallas import tpu as pltpu
from jax.sharding import PartitionSpec as P

SUB = 64
SWEEPS = 3
CAP = 4
EIG_LOW = 0.1
EIG_HIGH = 2.0
LANES = 128
PACK = 16
VMEM_BYTES = 67043328

MESH = pl.DeviceIdType.MESH
F32 = jnp.float32
BF16 = jnp.bfloat16


def iota(shape, dim):
    return lax.broadcasted_iota(jnp.int32, shape, dim)


def hi_dot(a, b, dims):
    return lax.dot_general(
        a, b, (dims, ((), ())), precision=lax.Precision.HIGHEST, preferred_element_type=F32
    )


def kernel(
    sizes,
    temp_hbm,
    cond_hbm,
    mass_hbm,
    dyn_hbm,
    leak_hbm,
    panel_hbm,
    place_hbm,
    block_hbm,
    tier_hbm,
    sens_hbm,
    out_hbm,
    power_hbm,
    panel_ref,
    place_ref,
    block_ref,
    tier_ref,
    sens_ref,
    out_ref,
    power_ref,
    temp,
    cond,
    mass,
    dyn,
    leak,
    note_send,
    note_recv,
    load_send,
    load_recv,
    dirs,
    faces,
    diag,
    inv,
    resid,
    edge_send,
    edge_recv,
    plane_recv,
    in_sem,
    out_sem,
    note_ssem,
    note_rsem,
    load_ssem,
    load_rsem,
    halo_ssem,
    halo_rsem,
):
    n_row, n_col, n_layer = sizes
    tiles = n_row * n_col
    tiers, rows, cols = temp.shape
    slots, cells = dyn.shape
    folds = PACK // CAP
    wide = cells // folds
    note_rows = note_send.shape[0] // tiles
    in_plane = (rows // SUB) * (cols // SUB)
    patches = tiers * in_plane
    bands = tiers * (rows // SUB)
    chunks = tiles * PACK // LANES

    my_row = lax.axis_index("row")
    my_col = lax.axis_index("col")
    my_layer = lax.axis_index("layer")
    me = my_row * n_col + my_col

    loads = [
        pltpu.make_async_copy(src, dst, in_sem.at[i])
        for i, (src, dst) in enumerate(
            (
                (panel_hbm, panel_ref),
                (place_hbm, place_ref),
                (block_hbm, block_ref),
                (tier_hbm, tier_ref),
                (sens_hbm, sens_ref),
                (temp_hbm, temp),
                (cond_hbm, cond),
                (dyn_hbm.at[0], dyn),
                (leak_hbm.at[0], leak),
                (mass_hbm, mass),
            )
        )
    ]
    for load in loads:
        load.start()

    def peer(step):
        other = lax.rem(me + step, tiles)
        return other, {"row": other // n_col, "col": lax.rem(other, n_col)}

    sides = (
        (my_layer > 0, {"layer": my_layer - 1}, 0),
        (my_layer < n_layer - 1, {"layer": my_layer + 1}, 1),
        (my_row > 0, {"row": my_row - 1}, 2),
        (my_row < n_row - 1, {"row": my_row + 1}, 3),
        (my_col > 0, {"col": my_col - 1}, 4),
        (my_col < n_col - 1, {"col": my_col + 1}, 5),
    )

    barrier = pltpu.get_barrier_semaphore()

    @pl.loop(1, tiles)
    def _(step):
        _, where = peer(step)
        pl.semaphore_signal(barrier, inc=1, device_id=where, device_id_type=MESH)

    for exists, where, side in sides[:2]:

        @pl.when(exists)
        def _(where=where):
            pl.semaphore_signal(barrier, inc=1, device_id=where, device_id_type=MESH)

    for turn in range(4):
        for exists, _, side in sides:

            @pl.when(jnp.logical_not(exists))
            def _(turn=turn, side=side):
                if side < 2:
                    plane_recv[turn, side] = jnp.zeros((rows, cols), F32)
                else:
                    edge_recv[turn, side - 2] = jnp.zeros(edge_recv.shape[2:], F32)

    lane_s = iota((slots, slots), 1)
    sub_s = iota((slots, slots), 0)
    eye = lane_s == sub_s

    def to_col(row):
        return jnp.sum(jnp.where(eye, jnp.broadcast_to(row, (slots, slots)), 0.0), axis=1, keepdims=True)

    def to_row(col):
        return jnp.sum(jnp.where(eye, jnp.broadcast_to(col, (slots, slots)), 0.0), axis=0, keepdims=True)

    for load in loads[:5]:
        load.wait()
    tgt_row = panel_ref[...].astype(F32)
    tgt_col = to_col(tgt_row)
    blk_row = block_ref[...].astype(F32)
    blk_col = to_col(blk_row)
    sub_col = to_col(place_ref[...].astype(F32))
    same_tile = tgt_col == tgt_row
    rank_col = jnp.sum(jnp.where(same_tile & (lane_s < sub_s), 1.0, 0.0), axis=1, keepdims=True)
    rank_row = jnp.sum(jnp.where(same_tile & (sub_s < lane_s), 1.0, 0.0), axis=0, keepdims=True)
    blocks = tier_ref.shape[1]
    of_block = blk_col == iota((slots, blocks), 1).astype(F32)
    tier_col = jnp.sum(jnp.where(of_block, tier_ref[...].astype(F32), 0.0), axis=1, keepdims=True)
    sens_col = jnp.sum(jnp.where(of_block, sens_ref[...], 0.0), axis=1, keepdims=True)
    pos_col = tier_col * in_plane + sub_col
    same_block = jnp.where(blk_col == blk_row, 1.0, 0.0)
    block_size = jnp.sum(same_block, axis=1, keepdims=True)

    offset = lax.rem(me * PACK, LANES)
    my_chunk = (me * PACK) // LANES
    rel = iota((slots, LANES), 1) - offset
    fits = (rel >= 0) & (rel < PACK) & ((rel & (CAP - 1)).astype(F32) == rank_col)
    place_lanes = jnp.where(fits, pos_col + 1.0, 0.0)
    note_i = iota((tiles * note_rows, slots), 0)
    to_tile = jnp.where(
        ((note_i // note_rows).astype(F32) == tgt_row) & (lax.rem(note_i, note_rows) == 1 + my_chunk),
        1.0,
        0.0,
    )
    places = jnp.dot(to_tile.astype(BF16), place_lanes.astype(BF16), preferred_element_type=F32)

    loads[5].wait()
    band_sums = jnp.concatenate(
        [
            jnp.sum(temp[t, b * SUB : (b + 1) * SUB, :], axis=0, keepdims=True)
            for t in range(tiers)
            for b in range(rows // SUB)
        ],
        axis=0,
    )
    lane_b = iota((bands, LANES), 1)
    sub_b = iota((bands, LANES), 0)
    means = jnp.zeros((1, LANES), F32)
    per_band = cols // SUB
    for part in range(per_band):
        total = jnp.sum(jnp.where(lane_b // SUB == part, band_sums, 0.0), axis=1, keepdims=True)
        means = means + jnp.sum(
            jnp.where(lane_b == sub_b * per_band + part, total, 0.0), axis=0, keepdims=True
        )
    means = means * (1.0 / (SUB * SUB))
    note_j = iota((tiles * note_rows, LANES), 0)
    note_send[...] = places + jnp.where(lax.rem(note_j, note_rows) == 0, means, 0.0)

    sub8 = iota((2 * tiers, LANES), 0)
    lane8 = iota((2 * tiers, LANES), 1)

    def halo_copy(turn, field, where, side, lands):
        if side < 2:
            src = field.at[0 if side == 0 else tiers - 1]
            dst = plane_recv.at[turn, lands]
        else:
            src = edge_send.at[turn, (side - 2) // 2]
            dst = edge_recv.at[turn, lands - 2]
        return pltpu.make_async_remote_copy(
            src_ref=src,
            dst_ref=dst,
            send_sem=halo_ssem.at[turn, side],
            recv_sem=halo_rsem.at[turn, lands],
            device_id=where,
            device_id_type=MESH,
        )

    def pack_edges(turn, field):
        for end in range(2):
            at = end * (rows - 1)
            for t in range(tiers):
                edge_send[turn, 0, end * tiers + t : end * tiers + t + 1, :] = field[t, at : at + 1, :]
        columns = jnp.zeros((2 * tiers, rows), F32)
        for t in range(tiers):
            pick = jnp.where(
                ((sub8 == t) & (lane8 == 0)) | ((sub8 == tiers + t) & (lane8 == cols - 1)), 1.0, 0.0
            )
            columns = columns + hi_dot(pick, field[t], ((1,), (1,)))
        edge_send[turn, 1] = columns

    def each_side(act):
        for exists, where, side in sides:
            pl.when(exists)(functools.partial(act, where, side))

    def start_halo(turn, field):
        each_side(lambda where, side: halo_copy(turn, field, where, side, side ^ 1).start())

    def wait_halo(turn, field):
        each_side(lambda where, side: halo_copy(turn, field, where, side, side).wait_recv())

    def end_halo(turn, field):
        each_side(lambda where, side: halo_copy(turn, field, where, side, side ^ 1).wait_send())

    row_i = iota((rows, cols), 0)
    col_i = iota((rows, cols), 1)
    sub16 = iota((4 * tiers, tiers * cols), 0)
    lane16 = iota((4 * tiers, tiers * cols), 1)
    put = jnp.where(
        ((lax.rem(lane16, cols) == 0) & (sub16 == tiers + lane16 // cols))
        | ((lax.rem(lane16, cols) == cols - 1) & (sub16 == 2 * tiers + lane16 // cols)),
        1.0,
        0.0,
    )

    def inside(field, t):
        v = field[t]
        none = jnp.zeros_like(v)
        low = none if t == 0 else field[t - 1]
        high = none if t == tiers - 1 else field[t + 1]
        north = jnp.where(row_i == 0, 0.0, pltpu.roll(v, 1, 0))
        south = jnp.where(row_i == rows - 1, 0.0, pltpu.roll(v, rows - 1, 0))
        west = jnp.where(col_i == 0, 0.0, pltpu.roll(v, 1, 1))
        east = jnp.where(col_i == cols - 1, 0.0, pltpu.roll(v, cols - 1, 1))
        return v, (low, high, north, south, west, east)

    def rims(turn):
        ends = jnp.concatenate([edge_recv[turn, 2], edge_recv[turn, 3]], axis=0)
        return hi_dot(ends, put, ((0,), (0,)))

    def apply_inside(field, t):
        v, around = inside(field, t)
        value = diag[t] * v
        for k in range(6):
            if not (k == 0 and t == 0 or k == 1 and t == tiers - 1):
                value = value - faces[k, t] * around[k]
        return value

    def add_beyond(turn):
        rim = rims(turn)
        resid[0] = resid[0] + faces[0, 0] * plane_recv[turn, 0]
        resid[tiers - 1] = resid[tiers - 1] + faces[1, tiers - 1] * plane_recv[turn, 1]
        for t in range(tiers):
            first, last = slice(0, 1), slice(rows - 1, rows)
            resid[t, first, :] = (
                resid[t, first, :] + faces[2, t, first, :] * edge_recv[turn, 0, tiers + t : tiers + t + 1, :]
            )
            resid[t, last, :] = (
                resid[t, last, :] + faces[3, t, last, :] * edge_recv[turn, 1, t : t + 1, :]
            )
            face = jnp.where(col_i == 0, faces[4, t], faces[5, t])
            resid[t] = resid[t] + face * rim[:, t * cols : (t + 1) * cols]

    beyond = (my_layer > 0).astype(jnp.int32) + (my_layer < n_layer - 1).astype(jnp.int32)
    pl.semaphore_wait(barrier, tiles - 1 + beyond)

    def note_copy(step):
        other, where = peer(step)
        return pltpu.make_async_remote_copy(
            src_ref=note_send.at[pl.ds(other * note_rows, note_rows), :],
            dst_ref=note_recv.at[pl.ds(me * note_rows, note_rows), :],
            send_sem=note_ssem.at[step],
            recv_sem=note_rsem.at[step],
            device_id=where,
            device_id_type=MESH,
        )

    def load_copy(step):
        other, where = peer(step)
        return pltpu.make_async_remote_copy(
            src_ref=load_send.at[pl.ds(other * PACK, PACK), :],
            dst_ref=load_recv.at[pl.ds(me * PACK, PACK), :],
            send_sem=load_ssem.at[step],
            recv_sem=load_rsem.at[step],
            device_id=where,
            device_id_type=MESH,
        )

    @pl.loop(1, tiles)
    def _(step):
        note_copy(step).start()

    own_note = pl.ds(pl.multiple_of(me * note_rows, note_rows), note_rows)
    own_copy = pltpu.make_async_copy(note_send.at[own_note, :], note_recv.at[own_note, :], note_rsem.at[0])
    own_copy.start()

    loads[6].wait()
    pack_edges(0, temp)
    start_halo(0, temp)
    pack_edges(1, cond)
    start_halo(1, cond)
    loads[7].wait()
    loads[8].wait()
    own_copy.wait()

    @pl.loop(1, tiles)
    def _(step):
        note_copy(step).wait_recv()

    note_k = iota((slots, tiles * note_rows), 1)
    from_tile = jnp.where(
        ((note_k // note_rows).astype(F32) == tgt_col) & (lax.rem(note_k, note_rows) == 0), 1.0, 0.0
    )
    tile_means = hi_dot(from_tile, note_recv[...], ((1,), (0,)))
    slot_mean = jnp.sum(
        jnp.where(iota((slots, LANES), 1).astype(F32) == pos_col, tile_means, 0.0), axis=1, keepdims=True
    )
    block_rise = jnp.sum(same_block * to_row(slot_mean), axis=1, keepdims=True) / block_size
    factor = jnp.exp(sens_col * block_rise)
    send_i = iota((tiles * PACK, slots), 0)
    goes = (
        (send_i // PACK) * CAP + lax.rem(send_i, CAP)
    ).astype(F32) == tgt_row * CAP + rank_row
    fold_i = lax.rem(send_i, PACK) // CAP
    gathered = jnp.zeros((tiles * PACK, wide), F32)
    for fold in range(folds):
        part = slice(fold * wide, (fold + 1) * wide)
        slot_power = (dyn[:, part].astype(F32) + factor * leak[:, part].astype(F32)).astype(BF16)
        pick = jnp.where(goes & (fold_i == fold), 1.0, 0.0).astype(BF16)
        gathered = gathered + jnp.dot(pick, slot_power, preferred_element_type=F32)
    load_send[...] = gathered.astype(BF16)

    @pl.loop(1, tiles)
    def _(step):
        load_copy(step).start()

    own_load = pl.ds(pl.multiple_of(me * PACK, PACK), PACK)
    own_move = pltpu.make_async_copy(load_send.at[own_load, :], load_recv.at[own_load, :], load_rsem.at[0])
    own_move.start()

    loads[9].wait()
    wait_halo(0, temp)
    wait_halo(1, cond)
    rim = rims(1)
    for t in range(tiers):
        c, (low, high, north, south, west, east) = inside(cond, t)
        here = rim[:, t * cols : (t + 1) * cols]
        low = plane_recv[1, 0] if t == 0 else low
        high = plane_recv[1, 1] if t == tiers - 1 else high
        north = jnp.where(row_i == 0, edge_recv[1, 0, tiers + t : tiers + t + 1, :], north)
        south = jnp.where(row_i == rows - 1, edge_recv[1, 1, t : t + 1, :], south)
        west = jnp.where(col_i == 0, here, west)
        east = jnp.where(col_i == cols - 1, here, east)
        total = mass[t]
        for k, beside in enumerate((low, high, north, south, west, east)):
            face = 0.5 * (c + beside)
            faces[k, t] = face
            total = total + face
        diag[t] = total
        inv[t] = 1.0 / total
    for t in range(tiers):
        resid[t] = mass[t] * temp[t] - apply_inside(temp, t)
    add_beyond(0)

    middle = (EIG_LOW + EIG_HIGH) / 2.0
    spread = (EIG_HIGH - EIG_LOW) / 2.0
    ratio = middle / spread
    weight = 1.0 / ratio

    sel_i = iota((folds * patches, LANES), 0)
    sel_j = iota((folds * patches, LANES), 1)
    sel_fold = sel_i // patches
    sel_in = lax.rem(sel_i, patches)
    sel_patch = lax.rem(sel_in, bands) * per_band + sel_in // bands
    fold_hit = sel_fold == lax.rem(sel_j, PACK) // CAP
    notes = note_recv[...]
    pickers = []
    for chunk in range(chunks):
        code = jnp.sum(jnp.where(lax.rem(note_j, note_rows) == 1 + chunk, notes, 0.0), axis=0, keepdims=True)
        pickers.append(
            jnp.where(fold_hit & (code == (sel_patch + 1).astype(F32)), 1.0, 0.0).astype(BF16)
        )

    own_move.wait()

    @pl.loop(1, tiles)
    def _(step):
        load_copy(step).wait_recv()

    footprint = jnp.zeros((folds * patches, wide), F32)
    for chunk in range(chunks):
        footprint = footprint + jnp.dot(
            pickers[chunk], load_recv[chunk * LANES : (chunk + 1) * LANES, :], preferred_element_type=F32
        )
    left = iota((bands, LANES), 1) < SUB
    for fold in range(folds):
        for k in range(wide // LANES):
            lanes = slice(k * LANES, (k + 1) * LANES)
            a = footprint[fold * patches : fold * patches + bands, lanes]
            b = footprint[fold * patches + bands : fold * patches + 2 * bands, lanes]
            at = 2 * (fold * (wide // LANES) + k)
            power_ref[pl.ds(at, bands, stride=SUB), :] = jnp.where(left, a, pltpu.roll(b, SUB, 1))
            power_ref[pl.ds(at + 1, bands, stride=SUB), :] = jnp.where(left, pltpu.roll(a, SUB, 1), b)

    power_out = pltpu.make_async_copy(power_ref, power_hbm, out_sem.at[1])
    power_out.start()
    for t in range(tiers):
        r = resid[t] + power_ref[t * rows : (t + 1) * rows, :]
        resid[t] = r
        dirs[0, t] = r * inv[t] * (1.0 / middle)
    for sweep in range(1, SWEEPS):
        field = dirs.at[sweep - 1]
        turn = 1 + sweep
        pack_edges(turn, field)
        start_halo(turn, field)
        weight_new = 1.0 / (2.0 * ratio - weight)
        for t in range(tiers):
            base = temp[t] if sweep == 1 else out_ref[t]
            out_ref[t] = base + field[t]
            resid[t] = resid[t] - apply_inside(field, t)
        wait_halo(turn, field)
        add_beyond(turn)
        for t in range(tiers):
            d = weight_new * weight * field[t] + (2.0 * weight_new / spread) * (resid[t] * inv[t])
            if sweep < SWEEPS - 1:
                dirs[sweep, t] = d
            else:
                out_ref[t] = out_ref[t] + d
        weight = weight_new
    out_copy = pltpu.make_async_copy(out_ref, out_hbm, out_sem.at[0])
    out_copy.start()

    end_halo(0, temp)
    end_halo(1, cond)
    for sweep in range(1, SWEEPS):
        end_halo(1 + sweep, dirs.at[sweep - 1])

    @pl.loop(1, tiles)
    def _(step):
        note_copy(step).wait_send()
        load_copy(step).wait_send()

    power_out.wait()
    out_copy.wait()


def shards(sizes, temp, cond, mass, dyn, leak, panel, place, block, tier, sens):
    tiers, rows, cols = temp.shape
    slots, cells = dyn.shape[1:]
    tiles = sizes[0] * sizes[1]
    folds = PACK // CAP
    note_rows = -(-(1 + tiles * PACK // LANES) // 8) * 8
    any_spec = pl.BlockSpec(memory_space=pl.ANY)
    grid = (tiers, rows, cols)
    dma = pltpu.SemaphoreType.DMA
    new, power = pl.pallas_call(
        functools.partial(kernel, sizes),
        out_shape=(
            jax.ShapeDtypeStruct(grid, F32),
            jax.ShapeDtypeStruct((tiers * rows, cols), F32),
        ),
        in_specs=[any_spec] * 10,
        out_specs=(any_spec, any_spec),
        scratch_shapes=[
            pltpu.VMEM((1, slots), jnp.int32),
            pltpu.VMEM((1, slots), jnp.int32),
            pltpu.VMEM((1, slots), jnp.int32),
            pltpu.VMEM(tier.shape, jnp.int32),
            pltpu.VMEM(sens.shape, F32),
            pltpu.VMEM(grid, F32),
            pltpu.VMEM((tiers * rows, cols), F32),
            pltpu.VMEM(grid, F32),
            pltpu.VMEM(grid, F32),
            pltpu.VMEM(grid, F32),
            pltpu.VMEM((slots, cells), BF16),
            pltpu.VMEM((slots, cells), BF16),
            pltpu.VMEM((tiles * note_rows, LANES), F32),
            pltpu.VMEM((tiles * note_rows, LANES), F32),
            pltpu.VMEM((tiles * PACK, cells // folds), BF16),
            pltpu.VMEM((tiles * PACK, cells // folds), BF16),
            pltpu.VMEM((SWEEPS - 1,) + grid, F32),
            pltpu.VMEM((6,) + grid, F32),
            pltpu.VMEM(grid, F32),
            pltpu.VMEM(grid, F32),
            pltpu.VMEM(grid, F32),
            pltpu.VMEM((SWEEPS + 1, 2, 2 * tiers, cols), F32),
            pltpu.VMEM((SWEEPS + 1, 4, 2 * tiers, cols), F32),
            pltpu.VMEM((SWEEPS + 1, 2, rows, cols), F32),
            dma((10,)),
            dma((2,)),
            dma((tiles,)),
            dma((tiles,)),
            dma((tiles,)),
            dma((tiles,)),
            dma((SWEEPS + 1, 6)),
            dma((SWEEPS + 1, 6)),
        ],
        compiler_params=pltpu.CompilerParams(
            collective_id=0, has_side_effects=True, vmem_limit_bytes=VMEM_BYTES
        ),
    )(temp, cond, mass, dyn, leak, panel.reshape(1, slots), place, block, tier, sens)
    return new, power.reshape(grid)


def solution(mesh):
    sizes = (mesh.shape["row"], mesh.shape["col"], mesh.shape["layer"])
    owner = ("row", "col", "layer")
    return jax.shard_map(
        functools.partial(shards, sizes),
        mesh=mesh,
        in_specs=(P("layer", "row", "col"),) * 3
        + (P(owner, None, None),) * 3
        + (P(owner, None),) * 4,
        out_specs=(P("layer", "row", "col"), P("layer", "row", "col")),
        check_vma=False,
    )
```

```python
import functools
import jax
import jax.numpy as jnp
from jax import lax
from jax.experimental import pallas as pl
from jax.experimental.pallas import tpu as pltpu
from jax.sharding import PartitionSpec as P

SUB = 64
SWEEPS = 3
CAP = 4
EIG_LOW = 0.1
EIG_HIGH = 2.0
LANES = 128
PACK = 16
VMEM_BYTES = 67043328

MESH = pl.DeviceIdType.MESH
F32 = jnp.float32
BF16 = jnp.bfloat16


def iota(shape, dim):
    return lax.broadcasted_iota(jnp.int32, shape, dim)


def hi_dot(a, b, dims):
    return lax.dot_general(
        a, b, (dims, ((), ())), precision=lax.Precision.HIGHEST, preferred_element_type=F32
    )


def div(x, n):
    if n & (n - 1):
        return x // n
    return lax.shift_right_logical(x, jnp.int32(n.bit_length() - 1))


def mod(x, n):
    if n & (n - 1):
        return lax.rem(x, n)
    return x & (n - 1)


def two_parts(x, axis):
    head = x.astype(BF16)
    return jnp.concatenate([head, (x - head.astype(F32)).astype(BF16)], axis=axis)


def kernel(
    sizes,
    temp_hbm,
    cond_hbm,
    mass_hbm,
    dyn_hbm,
    leak_hbm,
    panel_hbm,
    place_hbm,
    block_hbm,
    tier_hbm,
    sens_hbm,
    out_hbm,
    power_hbm,
    panel_ref,
    place_ref,
    block_ref,
    tier_ref,
    sens_ref,
    out_ref,
    power_ref,
    temp,
    cond,
    mass,
    dyn,
    leak,
    note_send,
    note_recv,
    load_send,
    load_recv,
    dirs,
    faces,
    diag,
    inv,
    resid,
    edge_send,
    edge_recv,
    plane_recv,
    in_sem,
    out_sem,
    note_ssem,
    note_rsem,
    load_ssem,
    load_rsem,
    halo_ssem,
    halo_rsem,
):
    n_row, n_col, n_layer = sizes
    tiles = n_row * n_col
    tiers, rows, cols = temp.shape
    slots, cells = dyn.shape
    folds = PACK // CAP
    wide = cells // folds
    note_rows = note_send.shape[0] // tiles
    in_plane = (rows // SUB) * (cols // SUB)
    patches = tiers * in_plane
    bands = tiers * (rows // SUB)
    chunks = tiles * PACK // LANES

    my_row = lax.axis_index("row")
    my_col = lax.axis_index("col")
    my_layer = lax.axis_index("layer")
    me = my_row * n_col + my_col

    loads = [
        pltpu.make_async_copy(src, dst, in_sem.at[i])
        for i, (src, dst) in enumerate(
            (
                (panel_hbm, panel_ref),
                (place_hbm, place_ref),
                (block_hbm, block_ref),
                (tier_hbm, tier_ref),
                (sens_hbm, sens_ref),
                (temp_hbm, temp),
                (cond_hbm, cond),
                (dyn_hbm.at[0], dyn),
                (leak_hbm.at[0], leak),
                (mass_hbm, mass),
            )
        )
    ]
    for load in loads:
        load.start()

    def peer(step):
        other = lax.rem(me + step, tiles)
        return other, {"row": other // n_col, "col": lax.rem(other, n_col)}

    sides = (
        (my_layer > 0, {"layer": my_layer - 1}, 0),
        (my_layer < n_layer - 1, {"layer": my_layer + 1}, 1),
        (my_row > 0, {"row": my_row - 1}, 2),
        (my_row < n_row - 1, {"row": my_row + 1}, 3),
        (my_col > 0, {"col": my_col - 1}, 4),
        (my_col < n_col - 1, {"col": my_col + 1}, 5),
    )

    barrier = pltpu.get_barrier_semaphore()

    @pl.loop(1, tiles)
    def _(step):
        _, where = peer(step)
        pl.semaphore_signal(barrier, inc=1, device_id=where, device_id_type=MESH)

    for exists, where, side in sides[:2]:

        @pl.when(exists)
        def _(where=where):
            pl.semaphore_signal(barrier, inc=1, device_id=where, device_id_type=MESH)

    for turn in range(4):
        for exists, _, side in sides:

            @pl.when(jnp.logical_not(exists))
            def _(turn=turn, side=side):
                if side < 2:
                    plane_recv[turn, side] = jnp.zeros((rows, cols), F32)
                else:
                    edge_recv[turn, side - 2] = jnp.zeros(edge_recv.shape[2:], F32)

    lane_s = iota((slots, slots), 1)
    sub_s = iota((slots, slots), 0)
    eye = lane_s == sub_s

    def to_col(row):
        return jnp.sum(jnp.where(eye, jnp.broadcast_to(row, (slots, slots)), 0.0), axis=1, keepdims=True)

    def to_row(col):
        return jnp.sum(jnp.where(eye, jnp.broadcast_to(col, (slots, slots)), 0.0), axis=0, keepdims=True)

    for load in loads[:5]:
        load.wait()
    tgt_row = panel_ref[...].astype(F32)
    tgt_col = to_col(tgt_row)
    blk_row = block_ref[...].astype(F32)
    blk_col = to_col(blk_row)
    sub_col = to_col(place_ref[...].astype(F32))
    same_tile = tgt_col == tgt_row
    rank_col = jnp.sum(jnp.where(same_tile & (lane_s < sub_s), 1.0, 0.0), axis=1, keepdims=True)
    rank_row = jnp.sum(jnp.where(same_tile & (sub_s < lane_s), 1.0, 0.0), axis=0, keepdims=True)
    blocks = tier_ref.shape[1]
    of_block = blk_col == iota((slots, blocks), 1).astype(F32)
    tier_col = jnp.sum(jnp.where(of_block, tier_ref[...].astype(F32), 0.0), axis=1, keepdims=True)
    sens_col = jnp.sum(jnp.where(of_block, sens_ref[...], 0.0), axis=1, keepdims=True)
    pos_col = tier_col * in_plane + sub_col
    same_block = jnp.where(blk_col == blk_row, 1.0, 0.0)
    block_size = jnp.sum(same_block, axis=1, keepdims=True)

    offset = lax.rem(me * PACK, LANES)
    my_chunk = (me * PACK) // LANES
    rel = iota((slots, LANES), 1) - offset
    fits = (rel >= 0) & (rel < PACK) & ((rel & (CAP - 1)).astype(F32) == rank_col)
    place_lanes = jnp.where(fits, pos_col + 1.0, 0.0)
    note_i = iota((tiles * note_rows, slots), 0)
    to_tile = jnp.where(
        (div(note_i, note_rows).astype(F32) == tgt_row) & (mod(note_i, note_rows) == 1 + my_chunk),
        1.0,
        0.0,
    )
    places = jnp.dot(to_tile.astype(BF16), place_lanes.astype(BF16), preferred_element_type=F32)

    loads[5].wait()
    band_sums = jnp.concatenate(
        [
            jnp.sum(temp[t, b * SUB : (b + 1) * SUB, :], axis=0, keepdims=True)
            for t in range(tiers)
            for b in range(rows // SUB)
        ],
        axis=0,
    )
    lane_b = iota((bands, LANES), 1)
    sub_b = iota((bands, LANES), 0)
    means = jnp.zeros((1, LANES), F32)
    per_band = cols // SUB
    for part in range(per_band):
        total = jnp.sum(jnp.where(div(lane_b, SUB) == part, band_sums, 0.0), axis=1, keepdims=True)
        means = means + jnp.sum(
            jnp.where(lane_b == sub_b * per_band + part, total, 0.0), axis=0, keepdims=True
        )
    means = means * (1.0 / (SUB * SUB))
    note_j = iota((tiles * note_rows, LANES), 0)
    note_send[...] = places + jnp.where(mod(note_j, note_rows) == 0, means, 0.0)

    sub8 = iota((2 * tiers, 2 * cols), 0)
    lane8 = mod(iota((2 * tiers, 2 * cols), 1), cols)
    picks = [
        jnp.where(
            ((sub8 == t) & (lane8 == 0)) | ((sub8 == tiers + t) & (lane8 == cols - 1)), 1.0, 0.0
        ).astype(BF16)
        for t in range(tiers)
    ]

    def halo_copy(turn, field, where, side, lands):
        if side < 2:
            src = field.at[0 if side == 0 else tiers - 1]
            dst = plane_recv.at[turn, lands]
        else:
            src = edge_send.at[turn, (side - 2) // 2]
            dst = edge_recv.at[turn, lands - 2]
        return pltpu.make_async_remote_copy(
            src_ref=src,
            dst_ref=dst,
            send_sem=halo_ssem.at[turn, side],
            recv_sem=halo_rsem.at[turn, lands],
            device_id=where,
            device_id_type=MESH,
        )

    def pack_edges(turn, field):
        for end in range(2):
            at = end * (rows - 1)
            for t in range(tiers):
                edge_send[turn, 0, end * tiers + t : end * tiers + t + 1, :] = field[t, at : at + 1, :]
        columns = jnp.zeros((2 * tiers, rows), F32)
        for t in range(tiers):
            columns = columns + lax.dot_general(
                picks[t], two_parts(field[t], 1), (((1,), (1,)), ((), ())), preferred_element_type=F32
            )
        edge_send[turn, 1] = columns

    def each_side(act):
        for exists, where, side in sides:
            pl.when(exists)(functools.partial(act, where, side))

    def start_halo(turn, field):
        each_side(lambda where, side: halo_copy(turn, field, where, side, side ^ 1).start())

    def wait_halo(turn, field):
        each_side(lambda where, side: halo_copy(turn, field, where, side, side).wait_recv())

    def end_halo(turn, field):
        each_side(lambda where, side: halo_copy(turn, field, where, side, side ^ 1).wait_send())

    row_i = iota((rows, cols), 0)
    col_i = iota((rows, cols), 1)
    sub16 = mod(iota((8 * tiers, tiers * cols), 0), 4 * tiers)
    lane16 = iota((8 * tiers, tiers * cols), 1)
    put = jnp.where(
        ((mod(lane16, cols) == 0) & (sub16 == tiers + div(lane16, cols)))
        | ((mod(lane16, cols) == cols - 1) & (sub16 == 2 * tiers + div(lane16, cols))),
        1.0,
        0.0,
    ).astype(BF16)

    def inside(field, t):
        v = field[t]
        none = jnp.zeros_like(v)
        low = none if t == 0 else field[t - 1]
        high = none if t == tiers - 1 else field[t + 1]
        north = jnp.where(row_i == 0, 0.0, pltpu.roll(v, 1, 0))
        south = jnp.where(row_i == rows - 1, 0.0, pltpu.roll(v, rows - 1, 0))
        west = jnp.where(col_i == 0, 0.0, pltpu.roll(v, 1, 1))
        east = jnp.where(col_i == cols - 1, 0.0, pltpu.roll(v, cols - 1, 1))
        return v, (low, high, north, south, west, east)

    def rims(turn):
        ends = jnp.concatenate([edge_recv[turn, 2], edge_recv[turn, 3]], axis=0)
        return lax.dot_general(
            two_parts(ends, 0), put, (((0,), (0,)), ((), ())), preferred_element_type=F32
        )

    def apply_inside(field, t):
        v, around = inside(field, t)
        value = diag[t] * v
        for k in range(6):
            if not (k == 0 and t == 0 or k == 1 and t == tiers - 1):
                value = value - faces[k, t] * around[k]
        return value

    def add_beyond(turn):
        rim = rims(turn)
        resid[0] = resid[0] + faces[0, 0] * plane_recv[turn, 0]
        resid[tiers - 1] = resid[tiers - 1] + faces[1, tiers - 1] * plane_recv[turn, 1]
        for t in range(tiers):
            first, last = slice(0, 1), slice(rows - 1, rows)
            resid[t, first, :] = (
                resid[t, first, :] + faces[2, t, first, :] * edge_recv[turn, 0, tiers + t : tiers + t + 1, :]
            )
            resid[t, last, :] = (
                resid[t, last, :] + faces[3, t, last, :] * edge_recv[turn, 1, t : t + 1, :]
            )
            face = jnp.where(col_i == 0, faces[4, t], faces[5, t])
            resid[t] = resid[t] + face * rim[:, t * cols : (t + 1) * cols]

    beyond = (my_layer > 0).astype(jnp.int32) + (my_layer < n_layer - 1).astype(jnp.int32)
    pl.semaphore_wait(barrier, tiles - 1 + beyond)

    def note_copy(step):
        other, where = peer(step)
        return pltpu.make_async_remote_copy(
            src_ref=note_send.at[pl.ds(other * note_rows, note_rows), :],
            dst_ref=note_recv.at[pl.ds(me * note_rows, note_rows), :],
            send_sem=note_ssem.at[step],
            recv_sem=note_rsem.at[step],
            device_id=where,
            device_id_type=MESH,
        )

    def load_copy(step):
        other, where = peer(step)
        return pltpu.make_async_remote_copy(
            src_ref=load_send.at[pl.ds(other * PACK, PACK), :],
            dst_ref=load_recv.at[pl.ds(me * PACK, PACK), :],
            send_sem=load_ssem.at[step],
            recv_sem=load_rsem.at[step],
            device_id=where,
            device_id_type=MESH,
        )

    @pl.loop(1, tiles)
    def _(step):
        note_copy(step).start()

    own_note = pl.ds(pl.multiple_of(me * note_rows, note_rows), note_rows)
    own_copy = pltpu.make_async_copy(note_send.at[own_note, :], note_recv.at[own_note, :], note_rsem.at[0])
    own_copy.start()

    loads[6].wait()
    pack_edges(0, temp)
    start_halo(0, temp)
    pack_edges(1, cond)
    start_halo(1, cond)
    loads[7].wait()
    loads[8].wait()
    note_k = iota((slots, tiles * note_rows), 1)
    from_tile = jnp.where(
        (div(note_k, note_rows).astype(F32) == tgt_col) & (mod(note_k, note_rows) == 0), 1.0, 0.0
    )
    at_place = iota((slots, LANES), 1).astype(F32) == pos_col
    send_i = iota((tiles * PACK, folds * slots), 0)
    send_j = iota((tiles * PACK, folds * slots), 1)
    slot_place = jnp.concatenate([tgt_row * CAP + rank_row] * folds, axis=1)
    goes = (div(send_i, PACK) * CAP + mod(send_i, CAP)).astype(F32) == slot_place
    pick = jnp.where(goes & (div(mod(send_i, PACK), CAP) == div(send_j, slots)), 1.0, 0.0).astype(BF16)
    own_copy.wait()

    @pl.loop(1, tiles)
    def _(step):
        note_copy(step).wait_recv()

    tile_means = hi_dot(from_tile, note_recv[...], ((1,), (0,)))
    slot_mean = jnp.sum(jnp.where(at_place, tile_means, 0.0), axis=1, keepdims=True)
    block_rise = jnp.sum(same_block * to_row(slot_mean), axis=1, keepdims=True) / block_size
    factor = jnp.exp(sens_col * block_rise)
    half = wide // 2
    for piece in range(2):
        slot_power = jnp.concatenate(
            [
                (
                    dyn[:, fold * wide + piece * half : fold * wide + (piece + 1) * half].astype(F32)
                    + factor
                    * leak[:, fold * wide + piece * half : fold * wide + (piece + 1) * half].astype(F32)
                ).astype(BF16)
                for fold in range(folds)
            ],
            axis=0,
        )
        load_send[:, piece * half : (piece + 1) * half] = jnp.dot(
            pick, slot_power, preferred_element_type=F32
        ).astype(BF16)

    @pl.loop(1, tiles)
    def _(step):
        load_copy(step).start()

    own_load = pl.ds(pl.multiple_of(me * PACK, PACK), PACK)
    own_move = pltpu.make_async_copy(load_send.at[own_load, :], load_recv.at[own_load, :], load_rsem.at[0])
    own_move.start()

    loads[9].wait()
    wait_halo(0, temp)
    wait_halo(1, cond)
    rim = rims(1)
    for t in range(tiers):
        c, (low, high, north, south, west, east) = inside(cond, t)
        here = rim[:, t * cols : (t + 1) * cols]
        low = plane_recv[1, 0] if t == 0 else low
        high = plane_recv[1, 1] if t == tiers - 1 else high
        north = jnp.where(row_i == 0, edge_recv[1, 0, tiers + t : tiers + t + 1, :], north)
        south = jnp.where(row_i == rows - 1, edge_recv[1, 1, t : t + 1, :], south)
        west = jnp.where(col_i == 0, here, west)
        east = jnp.where(col_i == cols - 1, here, east)
        total = mass[t]
        for k, beside in enumerate((low, high, north, south, west, east)):
            face = 0.5 * (c + beside)
            faces[k, t] = face
            total = total + face
        diag[t] = total
        inv[t] = 1.0 / total
    for t in range(tiers):
        resid[t] = mass[t] * temp[t] - apply_inside(temp, t)
    add_beyond(0)

    middle = (EIG_LOW + EIG_HIGH) / 2.0
    spread = (EIG_HIGH - EIG_LOW) / 2.0
    ratio = middle / spread
    weight = 1.0 / ratio

    sel_i = iota((folds * patches, LANES), 0)
    sel_j = iota((folds * patches, LANES), 1)
    sel_in = mod(sel_i, patches)
    sel_patch = mod(sel_in, bands) * per_band + div(sel_in, bands)
    fold_hit = div(sel_i, patches) == div(mod(sel_j, PACK), CAP)
    notes = note_recv[...]
    pickers = []
    for chunk in range(chunks):
        code = jnp.sum(jnp.where(mod(note_j, note_rows) == 1 + chunk, notes, 0.0), axis=0, keepdims=True)
        pickers.append(
            jnp.where(fold_hit & (code == (sel_patch + 1).astype(F32)), 1.0, 0.0).astype(BF16)
        )

    picker = jnp.concatenate(pickers, axis=1)
    own_move.wait()

    @pl.loop(1, tiles)
    def _(step):
        load_copy(step).wait_recv()

    footprint = jnp.dot(picker, load_recv[...], preferred_element_type=F32)
    left = iota((bands, LANES), 1) < SUB
    for fold in range(folds):
        for k in range(wide // LANES):
            lanes = slice(k * LANES, (k + 1) * LANES)
            a = footprint[fold * patches : fold * patches + bands, lanes]
            b = footprint[fold * patches + bands : fold * patches + 2 * bands, lanes]
            at = 2 * (fold * (wide // LANES) + k)
            power_ref[pl.ds(at, bands, stride=SUB), :] = jnp.where(left, a, pltpu.roll(b, SUB, 1))
            power_ref[pl.ds(at + 1, bands, stride=SUB), :] = jnp.where(left, pltpu.roll(a, SUB, 1), b)

    power_out = pltpu.make_async_copy(power_ref, power_hbm, out_sem.at[1])
    power_out.start()
    for t in range(tiers):
        r = resid[t] + power_ref[t * rows : (t + 1) * rows, :]
        resid[t] = r
        dirs[0, t] = r * inv[t] * (1.0 / middle)
    for sweep in range(1, SWEEPS):
        field = dirs.at[sweep - 1]
        turn = 1 + sweep
        pack_edges(turn, field)
        start_halo(turn, field)
        weight_new = 1.0 / (2.0 * ratio - weight)
        for t in range(tiers):
            base = temp[t] if sweep == 1 else out_ref[t]
            out_ref[t] = base + field[t]
            resid[t] = resid[t] - apply_inside(field, t)
        wait_halo(turn, field)
        add_beyond(turn)
        for t in range(tiers):
            d = weight_new * weight * field[t] + (2.0 * weight_new / spread) * (resid[t] * inv[t])
            if sweep < SWEEPS - 1:
                dirs[sweep, t] = d
            else:
                out_ref[t] = out_ref[t] + d
        weight = weight_new
    out_copy = pltpu.make_async_copy(out_ref, out_hbm, out_sem.at[0])
    out_copy.start()

    end_halo(0, temp)
    end_halo(1, cond)
    for sweep in range(1, SWEEPS):
        end_halo(1 + sweep, dirs.at[sweep - 1])

    @pl.loop(1, tiles)
    def _(step):
        note_copy(step).wait_send()
        load_copy(step).wait_send()

    power_out.wait()
    out_copy.wait()


def shards(sizes, temp, cond, mass, dyn, leak, panel, place, block, tier, sens):
    tiers, rows, cols = temp.shape
    slots, cells = dyn.shape[1:]
    tiles = sizes[0] * sizes[1]
    folds = PACK // CAP
    note_rows = -(-(1 + tiles * PACK // LANES) // 8) * 8
    any_spec = pl.BlockSpec(memory_space=pl.ANY)
    grid = (tiers, rows, cols)
    dma = pltpu.SemaphoreType.DMA
    new, power = pl.pallas_call(
        functools.partial(kernel, sizes),
        out_shape=(
            jax.ShapeDtypeStruct(grid, F32),
            jax.ShapeDtypeStruct((tiers * rows, cols), F32),
        ),
        in_specs=[any_spec] * 10,
        out_specs=(any_spec, any_spec),
        scratch_shapes=[
            pltpu.VMEM((1, slots), jnp.int32),
            pltpu.VMEM((1, slots), jnp.int32),
            pltpu.VMEM((1, slots), jnp.int32),
            pltpu.VMEM(tier.shape, jnp.int32),
            pltpu.VMEM(sens.shape, F32),
            pltpu.VMEM(grid, F32),
            pltpu.VMEM((tiers * rows, cols), F32),
            pltpu.VMEM(grid, F32),
            pltpu.VMEM(grid, F32),
            pltpu.VMEM(grid, F32),
            pltpu.VMEM((slots, cells), BF16),
            pltpu.VMEM((slots, cells), BF16),
            pltpu.VMEM((tiles * note_rows, LANES), F32),
            pltpu.VMEM((tiles * note_rows, LANES), F32),
            pltpu.VMEM((tiles * PACK, cells // folds), BF16),
            pltpu.VMEM((tiles * PACK, cells // folds), BF16),
            pltpu.VMEM((SWEEPS - 1,) + grid, F32),
            pltpu.VMEM((6,) + grid, F32),
            pltpu.VMEM(grid, F32),
            pltpu.VMEM(grid, F32),
            pltpu.VMEM(grid, F32),
            pltpu.VMEM((SWEEPS + 1, 2, 2 * tiers, cols), F32),
            pltpu.VMEM((SWEEPS + 1, 4, 2 * tiers, cols), F32),
            pltpu.VMEM((SWEEPS + 1, 2, rows, cols), F32),
            dma((10,)),
            dma((2,)),
            dma((tiles,)),
            dma((tiles,)),
            dma((tiles,)),
            dma((tiles,)),
            dma((SWEEPS + 1, 6)),
            dma((SWEEPS + 1, 6)),
        ],
        compiler_params=pltpu.CompilerParams(
            collective_id=0, has_side_effects=True, vmem_limit_bytes=VMEM_BYTES
        ),
    )(temp, cond, mass, dyn, leak, panel.reshape(1, slots), place, block, tier, sens)
    return new, power.reshape(grid)


def solution(mesh):
    sizes = (mesh.shape["row"], mesh.shape["col"], mesh.shape["layer"])
    owner = ("row", "col", "layer")
    return jax.shard_map(
        functools.partial(shards, sizes),
        mesh=mesh,
        in_specs=(P("layer", "row", "col"),) * 3
        + (P(owner, None, None),) * 3
        + (P(owner, None),) * 4,
        out_specs=(P("layer", "row", "col"), P("layer", "row", "col")),
        check_vma=False,
    )
```

```python
import functools
import jax
import jax.numpy as jnp
from jax import lax
from jax.experimental import pallas as pl
from jax.experimental.pallas import tpu as pltpu
from jax.sharding import PartitionSpec as P

SUB = 64
SWEEPS = 3
CAP = 4
EIG_LOW = 0.1
EIG_HIGH = 2.0
LANES = 128
PACK = 16
VMEM_BYTES = 67043328

MESH = pl.DeviceIdType.MESH
F32 = jnp.float32
BF16 = jnp.bfloat16


def iota(shape, dim):
    return lax.broadcasted_iota(jnp.int32, shape, dim)


def hi_dot(a, b, dims):
    return lax.dot_general(
        a, b, (dims, ((), ())), precision=lax.Precision.HIGHEST, preferred_element_type=F32
    )


def div(x, n):
    if n & (n - 1):
        return x // n
    return lax.shift_right_logical(x, jnp.int32(n.bit_length() - 1))


def mod(x, n):
    if n & (n - 1):
        return lax.rem(x, n)
    return x & (n - 1)


def two_parts(x, axis):
    head = x.astype(BF16)
    return jnp.concatenate([head, (x - head.astype(F32)).astype(BF16)], axis=axis)


def kernel(
    sizes,
    temp_hbm,
    cond_hbm,
    mass_hbm,
    dyn_hbm,
    leak_hbm,
    panel_hbm,
    place_hbm,
    block_hbm,
    tier_hbm,
    sens_hbm,
    out_hbm,
    power_hbm,
    panel_ref,
    place_ref,
    block_ref,
    tier_ref,
    sens_ref,
    out_ref,
    power_ref,
    temp,
    cond,
    mass,
    dyn,
    leak,
    note_send,
    note_recv,
    load_send,
    load_recv,
    dirs,
    faces,
    diag,
    inv,
    resid,
    edge_send,
    edge_recv,
    plane_recv,
    in_sem,
    out_sem,
    note_ssem,
    note_rsem,
    load_ssem,
    load_rsem,
    halo_ssem,
    halo_rsem,
):
    n_row, n_col, n_layer = sizes
    tiles = n_row * n_col
    tiers, rows, cols = temp.shape
    slots, cells = dyn.shape
    folds = PACK // CAP
    wide = cells // folds
    note_rows = note_send.shape[0] // tiles
    in_plane = (rows // SUB) * (cols // SUB)
    patches = tiers * in_plane
    bands = tiers * (rows // SUB)
    chunks = tiles * PACK // LANES

    my_row = lax.axis_index("row")
    my_col = lax.axis_index("col")
    my_layer = lax.axis_index("layer")
    me = my_row * n_col + my_col

    loads = [
        pltpu.make_async_copy(src, dst, in_sem.at[i])
        for i, (src, dst) in enumerate(
            (
                (panel_hbm, panel_ref),
                (place_hbm, place_ref),
                (block_hbm, block_ref),
                (tier_hbm, tier_ref),
                (sens_hbm, sens_ref),
                (temp_hbm, temp),
                (cond_hbm, cond),
                (dyn_hbm.at[0], dyn),
                (leak_hbm.at[0], leak),
                (mass_hbm, mass),
            )
        )
    ]
    for load in loads:
        load.start()

    def peer(step):
        other = lax.rem(me + step, tiles)
        return other, {"row": other // n_col, "col": lax.rem(other, n_col)}

    sides = (
        (my_layer > 0, {"layer": my_layer - 1}, 0),
        (my_layer < n_layer - 1, {"layer": my_layer + 1}, 1),
        (my_row > 0, {"row": my_row - 1}, 2),
        (my_row < n_row - 1, {"row": my_row + 1}, 3),
        (my_col > 0, {"col": my_col - 1}, 4),
        (my_col < n_col - 1, {"col": my_col + 1}, 5),
    )

    barrier = pltpu.get_barrier_semaphore()

    @pl.loop(1, tiles)
    def _(step):
        _, where = peer(step)
        pl.semaphore_signal(barrier, inc=1, device_id=where, device_id_type=MESH)

    for exists, where, side in sides[:2]:

        @pl.when(exists)
        def _(where=where):
            pl.semaphore_signal(barrier, inc=1, device_id=where, device_id_type=MESH)

    for turn in range(4):
        for exists, _, side in sides:

            @pl.when(jnp.logical_not(exists))
            def _(turn=turn, side=side):
                if side < 2:
                    plane_recv[turn, side] = jnp.zeros((rows, cols), F32)
                else:
                    edge_recv[turn, side - 2] = jnp.zeros(edge_recv.shape[2:], F32)

    lane_s = iota((slots, slots), 1)
    sub_s = iota((slots, slots), 0)
    eye = lane_s == sub_s

    def to_col(row):
        return jnp.sum(jnp.where(eye, jnp.broadcast_to(row, (slots, slots)), 0.0), axis=1, keepdims=True)

    def to_row(col):
        return jnp.sum(jnp.where(eye, jnp.broadcast_to(col, (slots, slots)), 0.0), axis=0, keepdims=True)

    for load in loads[:5]:
        load.wait()
    tgt_row = panel_ref[...].astype(F32)
    tgt_col = to_col(tgt_row)
    blk_row = block_ref[...].astype(F32)
    blk_col = to_col(blk_row)
    sub_col = to_col(place_ref[...].astype(F32))
    same_tile = tgt_col == tgt_row
    rank_col = jnp.sum(jnp.where(same_tile & (lane_s < sub_s), 1.0, 0.0), axis=1, keepdims=True)
    rank_row = jnp.sum(jnp.where(same_tile & (sub_s < lane_s), 1.0, 0.0), axis=0, keepdims=True)
    blocks = tier_ref.shape[1]
    of_block = blk_col == iota((slots, blocks), 1).astype(F32)
    tier_col = jnp.sum(jnp.where(of_block, tier_ref[...].astype(F32), 0.0), axis=1, keepdims=True)
    sens_col = jnp.sum(jnp.where(of_block, sens_ref[...], 0.0), axis=1, keepdims=True)
    pos_col = tier_col * in_plane + sub_col
    same_block = jnp.where(blk_col == blk_row, 1.0, 0.0)
    block_size = jnp.sum(same_block, axis=1, keepdims=True)

    offset = lax.rem(me * PACK, LANES)
    my_chunk = (me * PACK) // LANES
    rel = iota((slots, LANES), 1) - offset
    fits = (rel >= 0) & (rel < PACK) & ((rel & (CAP - 1)).astype(F32) == rank_col)
    place_lanes = jnp.where(fits, pos_col + 1.0, 0.0)
    note_i = iota((tiles * note_rows, slots), 0)
    to_tile = jnp.where(
        (div(note_i, note_rows).astype(F32) == tgt_row) & (mod(note_i, note_rows) == 1 + my_chunk),
        1.0,
        0.0,
    )
    places = jnp.dot(to_tile.astype(BF16), place_lanes.astype(BF16), preferred_element_type=F32)

    loads[5].wait()
    band_sums = jnp.concatenate(
        [
            jnp.sum(temp[t, b * SUB : (b + 1) * SUB, :], axis=0, keepdims=True)
            for t in range(tiers)
            for b in range(rows // SUB)
        ],
        axis=0,
    )
    lane_b = iota((bands, LANES), 1)
    sub_b = iota((bands, LANES), 0)
    means = jnp.zeros((1, LANES), F32)
    per_band = cols // SUB
    for part in range(per_band):
        total = jnp.sum(jnp.where(div(lane_b, SUB) == part, band_sums, 0.0), axis=1, keepdims=True)
        means = means + jnp.sum(
            jnp.where(lane_b == sub_b * per_band + part, total, 0.0), axis=0, keepdims=True
        )
    means = means * (1.0 / (SUB * SUB))
    note_j = iota((tiles * note_rows, LANES), 0)
    note_send[...] = places + jnp.where(mod(note_j, note_rows) == 0, means, 0.0)

    sub8 = iota((2 * tiers, 2 * cols), 0)
    lane8 = mod(iota((2 * tiers, 2 * cols), 1), cols)
    picks = [
        jnp.where(
            ((sub8 == t) & (lane8 == 0)) | ((sub8 == tiers + t) & (lane8 == cols - 1)), 1.0, 0.0
        ).astype(BF16)
        for t in range(tiers)
    ]

    def halo_copy(turn, field, where, side, lands):
        if side < 2:
            src = field.at[0 if side == 0 else tiers - 1]
            dst = plane_recv.at[turn, lands]
        else:
            src = edge_send.at[turn, (side - 2) // 2]
            dst = edge_recv.at[turn, lands - 2]
        return pltpu.make_async_remote_copy(
            src_ref=src,
            dst_ref=dst,
            send_sem=halo_ssem.at[turn, side],
            recv_sem=halo_rsem.at[turn, lands],
            device_id=where,
            device_id_type=MESH,
        )

    def pack_rows(turn, field):
        for end in range(2):
            at = end * (rows - 1)
            for t in range(tiers):
                edge_send[turn, 0, end * tiers + t : end * tiers + t + 1, :] = field[t, at : at + 1, :]

    def pack_columns(turn, field):
        columns = jnp.zeros((2 * tiers, rows), F32)
        for t in range(tiers):
            columns = columns + lax.dot_general(
                picks[t], two_parts(field[t], 1), (((1,), (1,)), ((), ())), preferred_element_type=F32
            )
        edge_send[turn, 1] = columns

    def each_side(act, which=sides):
        for exists, where, side in which:
            pl.when(exists)(functools.partial(act, where, side))

    def start_halo(turn, field):
        def start(where, side):
            halo_copy(turn, field, where, side, side ^ 1).start()

        pack_rows(turn, field)
        each_side(start, sides[2:4])
        each_side(start, sides[:2])
        pack_columns(turn, field)
        each_side(start, sides[4:])

    def wait_halo(turn, field):
        each_side(lambda where, side: halo_copy(turn, field, where, side, side).wait_recv())

    def end_halo(turn, field):
        each_side(lambda where, side: halo_copy(turn, field, where, side, side ^ 1).wait_send())

    row_i = iota((rows, cols), 0)
    col_i = iota((rows, cols), 1)
    sub16 = mod(iota((8 * tiers, tiers * cols), 0), 4 * tiers)
    lane16 = iota((8 * tiers, tiers * cols), 1)
    put = jnp.where(
        ((mod(lane16, cols) == 0) & (sub16 == tiers + div(lane16, cols)))
        | ((mod(lane16, cols) == cols - 1) & (sub16 == 2 * tiers + div(lane16, cols))),
        1.0,
        0.0,
    ).astype(BF16)

    def inside(field, t):
        v = field[t]
        none = jnp.zeros_like(v)
        low = none if t == 0 else field[t - 1]
        high = none if t == tiers - 1 else field[t + 1]
        north = jnp.where(row_i == 0, 0.0, pltpu.roll(v, 1, 0))
        south = jnp.where(row_i == rows - 1, 0.0, pltpu.roll(v, rows - 1, 0))
        west = jnp.where(col_i == 0, 0.0, pltpu.roll(v, 1, 1))
        east = jnp.where(col_i == cols - 1, 0.0, pltpu.roll(v, cols - 1, 1))
        return v, (low, high, north, south, west, east)

    def rims(turn):
        ends = jnp.concatenate([edge_recv[turn, 2], edge_recv[turn, 3]], axis=0)
        return lax.dot_general(
            two_parts(ends, 0), put, (((0,), (0,)), ((), ())), preferred_element_type=F32
        )

    def apply_inside(field, t):
        v, around = inside(field, t)
        value = diag[t] * v
        for k in range(6):
            if not (k == 0 and t == 0 or k == 1 and t == tiers - 1):
                value = value - faces[k, t] * around[k]
        return value

    def add_beyond(turn):
        rim = rims(turn)
        resid[0] = resid[0] + faces[0, 0] * plane_recv[turn, 0]
        resid[tiers - 1] = resid[tiers - 1] + faces[1, tiers - 1] * plane_recv[turn, 1]
        for t in range(tiers):
            first, last = slice(0, 1), slice(rows - 1, rows)
            resid[t, first, :] = (
                resid[t, first, :] + faces[2, t, first, :] * edge_recv[turn, 0, tiers + t : tiers + t + 1, :]
            )
            resid[t, last, :] = (
                resid[t, last, :] + faces[3, t, last, :] * edge_recv[turn, 1, t : t + 1, :]
            )
            face = jnp.where(col_i == 0, faces[4, t], faces[5, t])
            resid[t] = resid[t] + face * rim[:, t * cols : (t + 1) * cols]

    beyond = (my_layer > 0).astype(jnp.int32) + (my_layer < n_layer - 1).astype(jnp.int32)
    pl.semaphore_wait(barrier, tiles - 1 + beyond)

    def note_copy(step):
        other, where = peer(step)
        return pltpu.make_async_remote_copy(
            src_ref=note_send.at[pl.ds(other * note_rows, note_rows), :],
            dst_ref=note_recv.at[pl.ds(me * note_rows, note_rows), :],
            send_sem=note_ssem.at[step],
            recv_sem=note_rsem.at[step],
            device_id=where,
            device_id_type=MESH,
        )

    def load_copy(other, lands):
        return pltpu.make_async_remote_copy(
            src_ref=load_send.at[pl.ds(other * PACK, PACK), :],
            dst_ref=load_recv.at[pl.ds(me * PACK, PACK), :],
            send_sem=load_ssem.at[other],
            recv_sem=load_rsem.at[lands],
            device_id={"row": div(other, n_col), "col": mod(other, n_col)},
            device_id_type=MESH,
        )

    @pl.loop(1, tiles)
    def _(step):
        note_copy(step).start()

    own_note = pl.ds(pl.multiple_of(me * note_rows, note_rows), note_rows)
    own_copy = pltpu.make_async_copy(note_send.at[own_note, :], note_recv.at[own_note, :], note_rsem.at[0])
    own_copy.start()

    loads[6].wait()
    start_halo(0, temp)
    start_halo(1, cond)
    loads[7].wait()
    loads[8].wait()
    note_k = iota((slots, tiles * note_rows), 1)
    from_tile = jnp.where(
        (div(note_k, note_rows).astype(F32) == tgt_col) & (mod(note_k, note_rows) == 0), 1.0, 0.0
    )
    at_place = iota((slots, LANES), 1).astype(F32) == pos_col
    send_i = iota((tiles * PACK, folds * slots), 0)
    send_j = iota((tiles * PACK, folds * slots), 1)
    slot_place = jnp.concatenate([tgt_row * CAP + rank_row] * folds, axis=1)
    goes = (div(send_i, PACK) * CAP + mod(send_i, CAP)).astype(F32) == slot_place
    pick = jnp.where(goes & (div(mod(send_i, PACK), CAP) == div(send_j, slots)), 1.0, 0.0).astype(BF16)
    own_copy.wait()

    @pl.loop(1, tiles)
    def _(step):
        note_copy(step).wait_recv()

    tile_means = hi_dot(from_tile, note_recv[...], ((1,), (0,)))
    slot_mean = jnp.sum(jnp.where(at_place, tile_means, 0.0), axis=1, keepdims=True)
    block_rise = jnp.sum(same_block * to_row(slot_mean), axis=1, keepdims=True) / block_size
    factor = jnp.exp(sens_col * block_rise)
    half = wide // 2
    for piece in range(2):
        slot_power = jnp.concatenate(
            [
                (
                    dyn[:, fold * wide + piece * half : fold * wide + (piece + 1) * half].astype(F32)
                    + factor
                    * leak[:, fold * wide + piece * half : fold * wide + (piece + 1) * half].astype(F32)
                ).astype(BF16)
                for fold in range(folds)
            ],
            axis=0,
        )
        load_send[:, piece * half : (piece + 1) * half] = jnp.dot(
            pick, slot_power, preferred_element_type=F32
        ).astype(BF16)

    @pl.loop(0, tiles)
    def _(step):
        nth = div(step, n_row)
        far = jnp.where(my_col < n_col // 2, n_col - 1 - nth, nth)
        other = lax.rem(my_row + lax.rem(step, n_row), n_row) * n_col + far

        @pl.when(other != me)
        def _():
            load_copy(other, me).start()

    own_load = pl.ds(pl.multiple_of(me * PACK, PACK), PACK)
    own_move = pltpu.make_async_copy(load_send.at[own_load, :], load_recv.at[own_load, :], load_rsem.at[me])
    own_move.start()

    loads[9].wait()
    wait_halo(0, temp)
    wait_halo(1, cond)
    rim = rims(1)
    for t in range(tiers):
        c, (low, high, north, south, west, east) = inside(cond, t)
        here = rim[:, t * cols : (t + 1) * cols]
        low = plane_recv[1, 0] if t == 0 else low
        high = plane_recv[1, 1] if t == tiers - 1 else high
        north = jnp.where(row_i == 0, edge_recv[1, 0, tiers + t : tiers + t + 1, :], north)
        south = jnp.where(row_i == rows - 1, edge_recv[1, 1, t : t + 1, :], south)
        west = jnp.where(col_i == 0, here, west)
        east = jnp.where(col_i == cols - 1, here, east)
        total = mass[t]
        for k, beside in enumerate((low, high, north, south, west, east)):
            face = 0.5 * (c + beside)
            faces[k, t] = face
            total = total + face
        diag[t] = total
        inv[t] = 1.0 / total
    for t in range(tiers):
        resid[t] = mass[t] * temp[t] - apply_inside(temp, t)
    add_beyond(0)

    middle = (EIG_LOW + EIG_HIGH) / 2.0
    spread = (EIG_HIGH - EIG_LOW) / 2.0
    ratio = middle / spread
    weight = 1.0 / ratio

    sel_i = iota((folds * patches, LANES), 0)
    sel_j = iota((folds * patches, LANES), 1)
    sel_in = mod(sel_i, patches)
    sel_patch = mod(sel_in, bands) * per_band + div(sel_in, bands)
    fold_hit = div(sel_i, patches) == div(mod(sel_j, PACK), CAP)
    notes = note_recv[...]
    pickers = []
    for chunk in range(chunks):
        code = jnp.sum(jnp.where(mod(note_j, note_rows) == 1 + chunk, notes, 0.0), axis=0, keepdims=True)
        pickers.append(
            jnp.where(fold_hit & (code == (sel_patch + 1).astype(F32)), 1.0, 0.0).astype(BF16)
        )

    picker = jnp.concatenate(pickers, axis=1)
    own_move.wait()

    @pl.loop(1, tiles)
    def _(step):
        other, _ = peer(step)
        load_copy(other, other).wait_recv()

    footprint = jnp.dot(picker, load_recv[...], preferred_element_type=F32)
    left = iota((bands, LANES), 1) < SUB
    for fold in range(folds):
        for k in range(wide // LANES):
            lanes = slice(k * LANES, (k + 1) * LANES)
            a = footprint[fold * patches : fold * patches + bands, lanes]
            b = footprint[fold * patches + bands : fold * patches + 2 * bands, lanes]
            at = 2 * (fold * (wide // LANES) + k)
            power_ref[pl.ds(at, bands, stride=SUB), :] = jnp.where(left, a, pltpu.roll(b, SUB, 1))
            power_ref[pl.ds(at + 1, bands, stride=SUB), :] = jnp.where(left, pltpu.roll(a, SUB, 1), b)

    power_out = pltpu.make_async_copy(power_ref, power_hbm, out_sem.at[1])
    power_out.start()
    for t in range(tiers):
        r = resid[t] + power_ref[t * rows : (t + 1) * rows, :]
        resid[t] = r
        dirs[0, t] = r * inv[t] * (1.0 / middle)
    for sweep in range(1, SWEEPS):
        field = dirs.at[sweep - 1]
        turn = 1 + sweep
        start_halo(turn, field)
        weight_new = 1.0 / (2.0 * ratio - weight)
        for t in range(tiers):
            base = temp[t] if sweep == 1 else out_ref[t]
            out_ref[t] = base + field[t]
            resid[t] = resid[t] - apply_inside(field, t)
        wait_halo(turn, field)
        add_beyond(turn)
        for t in range(tiers):
            d = weight_new * weight * field[t] + (2.0 * weight_new / spread) * (resid[t] * inv[t])
            if sweep < SWEEPS - 1:
                dirs[sweep, t] = d
            else:
                out_ref[t] = out_ref[t] + d
        weight = weight_new
    out_copy = pltpu.make_async_copy(out_ref, out_hbm, out_sem.at[0])
    out_copy.start()

    end_halo(0, temp)
    end_halo(1, cond)
    for sweep in range(1, SWEEPS):
        end_halo(1 + sweep, dirs.at[sweep - 1])

    @pl.loop(1, tiles)
    def _(step):
        note_copy(step).wait_send()
        other, _ = peer(step)
        load_copy(other, me).wait_send()

    power_out.wait()
    out_copy.wait()


def hand_over(new, power, new_out, power_out, held, sem):
    pairs = ((power, power_out), (new, new_out))
    takes = [pltpu.make_async_copy(src, held.at[i], sem.at[0, i]) for i, (src, _) in enumerate(pairs)]
    gives = [pltpu.make_async_copy(held.at[i], dst, sem.at[1, i]) for i, (_, dst) in enumerate(pairs)]
    for take in takes:
        take.start()
    for take, give in zip(takes, gives):
        take.wait()
        give.start()
    for give in gives:
        give.wait()


def shards(sizes, temp, cond, mass, dyn, leak, panel, place, block, tier, sens):
    tiers, rows, cols = temp.shape
    slots, cells = dyn.shape[1:]
    tiles = sizes[0] * sizes[1]
    folds = PACK // CAP
    note_rows = -(-(1 + tiles * PACK // LANES) // 8) * 8
    any_spec = pl.BlockSpec(memory_space=pl.ANY)
    grid = (tiers, rows, cols)
    dma = pltpu.SemaphoreType.DMA
    new, power = pl.pallas_call(
        functools.partial(kernel, sizes),
        out_shape=(
            jax.ShapeDtypeStruct(grid, F32),
            jax.ShapeDtypeStruct((tiers * rows, cols), F32),
        ),
        in_specs=[any_spec] * 10,
        out_specs=(any_spec, any_spec),
        scratch_shapes=[
            pltpu.VMEM((1, slots), jnp.int32),
            pltpu.VMEM((1, slots), jnp.int32),
            pltpu.VMEM((1, slots), jnp.int32),
            pltpu.VMEM(tier.shape, jnp.int32),
            pltpu.VMEM(sens.shape, F32),
            pltpu.VMEM(grid, F32),
            pltpu.VMEM((tiers * rows, cols), F32),
            pltpu.VMEM(grid, F32),
            pltpu.VMEM(grid, F32),
            pltpu.VMEM(grid, F32),
            pltpu.VMEM((slots, cells), BF16),
            pltpu.VMEM((slots, cells), BF16),
            pltpu.VMEM((tiles * note_rows, LANES), F32),
            pltpu.VMEM((tiles * note_rows, LANES), F32),
            pltpu.VMEM((tiles * PACK, cells // folds), BF16),
            pltpu.VMEM((tiles * PACK, cells // folds), BF16),
            pltpu.VMEM((SWEEPS - 1,) + grid, F32),
            pltpu.VMEM((6,) + grid, F32),
            pltpu.VMEM(grid, F32),
            pltpu.VMEM(grid, F32),
            pltpu.VMEM(grid, F32),
            pltpu.VMEM((SWEEPS + 1, 2, 2 * tiers, cols), F32),
            pltpu.VMEM((SWEEPS + 1, 4, 2 * tiers, cols), F32),
            pltpu.VMEM((SWEEPS + 1, 2, rows, cols), F32),
            dma((10,)),
            dma((2,)),
            dma((tiles,)),
            dma((tiles,)),
            dma((tiles,)),
            dma((tiles,)),
            dma((SWEEPS + 1, 6)),
            dma((SWEEPS + 1, 6)),
        ],
        compiler_params=pltpu.CompilerParams(
            collective_id=0, has_side_effects=True, vmem_limit_bytes=VMEM_BYTES
        ),
    )(temp, cond, mass, dyn, leak, panel.reshape(1, slots), place, block, tier, sens)
    return pl.pallas_call(
        hand_over,
        out_shape=(jax.ShapeDtypeStruct(grid, F32),) * 2,
        in_specs=[any_spec] * 2,
        out_specs=(any_spec, any_spec),
        scratch_shapes=[pltpu.VMEM((2,) + grid, F32), dma((2, 2))],
        compiler_params=pltpu.CompilerParams(vmem_limit_bytes=VMEM_BYTES),
    )(new, power.reshape(grid))


def solution(mesh):
    sizes = (mesh.shape["row"], mesh.shape["col"], mesh.shape["layer"])
    owner = ("row", "col", "layer")
    return jax.shard_map(
        functools.partial(shards, sizes),
        mesh=mesh,
        in_specs=(P("layer", "row", "col"),) * 3
        + (P(owner, None, None),) * 3
        + (P(owner, None),) * 4,
        out_specs=(P("layer", "row", "col"), P("layer", "row", "col")),
        check_vma=False,
    )
```

```python
import functools
import jax
import jax.numpy as jnp
from jax import lax
from jax.experimental import pallas as pl
from jax.experimental.pallas import tpu as pltpu
from jax.sharding import PartitionSpec as P

SUB = 64
SWEEPS = 3
CAP = 4
EIG_LOW = 0.1
EIG_HIGH = 2.0
LANES = 128
PACK = 16
VMEM_BYTES = 67043328

MESH = pl.DeviceIdType.MESH
F32 = jnp.float32
BF16 = jnp.bfloat16


def iota(shape, dim):
    return lax.broadcasted_iota(jnp.int32, shape, dim)


def hi_dot(a, b, dims):
    return lax.dot_general(
        a, b, (dims, ((), ())), precision=lax.Precision.HIGHEST, preferred_element_type=F32
    )


def div(x, n):
    if n & (n - 1):
        return x // n
    return lax.shift_right_logical(x, jnp.int32(n.bit_length() - 1))


def mod(x, n):
    if n & (n - 1):
        return lax.rem(x, n)
    return x & (n - 1)


def two_parts(x, axis):
    head = x.astype(BF16)
    return jnp.concatenate([head, (x - head.astype(F32)).astype(BF16)], axis=axis)


def kernel(
    sizes,
    temp_hbm,
    cond_hbm,
    mass_hbm,
    dyn_hbm,
    leak_hbm,
    panel_hbm,
    place_hbm,
    block_hbm,
    tier_hbm,
    sens_hbm,
    out_hbm,
    power_hbm,
    panel_ref,
    place_ref,
    block_ref,
    tier_ref,
    sens_ref,
    out_ref,
    power_ref,
    temp,
    cond,
    mass,
    dyn,
    leak,
    note_send,
    note_recv,
    load_send,
    load_recv,
    dirs,
    faces,
    diag,
    inv,
    resid,
    edge_send,
    edge_recv,
    plane_recv,
    in_sem,
    out_sem,
    note_ssem,
    note_rsem,
    load_ssem,
    load_rsem,
    halo_ssem,
    halo_rsem,
):
    n_row, n_col, n_layer = sizes
    tiles = n_row * n_col
    tiers, rows, cols = temp.shape
    slots, cells = dyn.shape
    folds = PACK // CAP
    wide = cells // folds
    note_rows = note_send.shape[0] // tiles
    in_plane = (rows // SUB) * (cols // SUB)
    patches = tiers * in_plane
    bands = tiers * (rows // SUB)
    chunks = tiles * PACK // LANES

    my_row = lax.axis_index("row")
    my_col = lax.axis_index("col")
    my_layer = lax.axis_index("layer")
    me = my_row * n_col + my_col

    loads = [
        pltpu.make_async_copy(src, dst, in_sem.at[i])
        for i, (src, dst) in enumerate(
            (
                (panel_hbm, panel_ref),
                (place_hbm, place_ref),
                (block_hbm, block_ref),
                (tier_hbm, tier_ref),
                (sens_hbm, sens_ref),
                (temp_hbm, temp),
                (cond_hbm, cond),
                (dyn_hbm.at[0], dyn),
                (leak_hbm.at[0], leak),
                (mass_hbm, mass),
            )
        )
    ]
    for load in loads:
        load.start()

    def peer(step):
        other = lax.rem(me + step, tiles)
        return other, {"row": other // n_col, "col": lax.rem(other, n_col)}

    sides = (
        (my_layer > 0, {"layer": my_layer - 1}, 0),
        (my_layer < n_layer - 1, {"layer": my_layer + 1}, 1),
        (my_row > 0, {"row": my_row - 1}, 2),
        (my_row < n_row - 1, {"row": my_row + 1}, 3),
        (my_col > 0, {"col": my_col - 1}, 4),
        (my_col < n_col - 1, {"col": my_col + 1}, 5),
    )

    barrier = pltpu.get_barrier_semaphore()

    @pl.loop(1, tiles)
    def _(step):
        _, where = peer(step)
        pl.semaphore_signal(barrier, inc=1, device_id=where, device_id_type=MESH)

    for exists, where, side in sides[:2]:

        @pl.when(exists)
        def _(where=where):
            pl.semaphore_signal(barrier, inc=1, device_id=where, device_id_type=MESH)

    for turn in range(4):
        for exists, _, side in sides:

            @pl.when(jnp.logical_not(exists))
            def _(turn=turn, side=side):
                if side < 2:
                    plane_recv[turn, side] = jnp.zeros((rows, cols), F32)
                else:
                    edge_recv[turn, side - 2] = jnp.zeros(edge_recv.shape[2:], F32)

    lane_s = iota((slots, slots), 1)
    sub_s = iota((slots, slots), 0)
    eye = lane_s == sub_s

    def to_col(row):
        return jnp.sum(jnp.where(eye, jnp.broadcast_to(row, (slots, slots)), 0.0), axis=1, keepdims=True)

    def to_row(col):
        return jnp.sum(jnp.where(eye, jnp.broadcast_to(col, (slots, slots)), 0.0), axis=0, keepdims=True)

    for load in loads[:5]:
        load.wait()
    tgt_row = panel_ref[...].astype(F32)
    tgt_col = to_col(tgt_row)
    blk_row = block_ref[...].astype(F32)
    blk_col = to_col(blk_row)
    sub_col = to_col(place_ref[...].astype(F32))
    same_tile = tgt_col == tgt_row
    rank_col = jnp.sum(jnp.where(same_tile & (lane_s < sub_s), 1.0, 0.0), axis=1, keepdims=True)
    rank_row = jnp.sum(jnp.where(same_tile & (sub_s < lane_s), 1.0, 0.0), axis=0, keepdims=True)
    blocks = tier_ref.shape[1]
    of_block = blk_col == iota((slots, blocks), 1).astype(F32)
    tier_col = jnp.sum(jnp.where(of_block, tier_ref[...].astype(F32), 0.0), axis=1, keepdims=True)
    sens_col = jnp.sum(jnp.where(of_block, sens_ref[...], 0.0), axis=1, keepdims=True)
    pos_col = tier_col * in_plane + sub_col
    same_block = jnp.where(blk_col == blk_row, 1.0, 0.0)
    block_size = jnp.sum(same_block, axis=1, keepdims=True)

    offset = lax.rem(me * PACK, LANES)
    my_chunk = (me * PACK) // LANES
    rel = iota((slots, LANES), 1) - offset
    fits = (rel >= 0) & (rel < PACK) & ((rel & (CAP - 1)).astype(F32) == rank_col)
    place_lanes = jnp.where(fits, pos_col + 1.0, 0.0)
    note_i = iota((tiles * note_rows, slots), 0)
    to_tile = jnp.where(
        (div(note_i, note_rows).astype(F32) == tgt_row) & (mod(note_i, note_rows) == 1 + my_chunk),
        1.0,
        0.0,
    )
    places = jnp.dot(to_tile.astype(BF16), place_lanes.astype(BF16), preferred_element_type=F32)

    loads[5].wait()
    band_sums = jnp.concatenate(
        [
            jnp.sum(temp[t, b * SUB : (b + 1) * SUB, :], axis=0, keepdims=True)
            for t in range(tiers)
            for b in range(rows // SUB)
        ],
        axis=0,
    )
    lane_b = iota((bands, LANES), 1)
    sub_b = iota((bands, LANES), 0)
    means = jnp.zeros((1, LANES), F32)
    per_band = cols // SUB
    for part in range(per_band):
        total = jnp.sum(jnp.where(div(lane_b, SUB) == part, band_sums, 0.0), axis=1, keepdims=True)
        means = means + jnp.sum(
            jnp.where(lane_b == sub_b * per_band + part, total, 0.0), axis=0, keepdims=True
        )
    means = means * (1.0 / (SUB * SUB))
    note_j = iota((tiles * note_rows, LANES), 0)
    note_send[...] = places + jnp.where(mod(note_j, note_rows) == 0, means, 0.0)

    sub8 = iota((2 * tiers, 2 * cols), 0)
    lane8 = mod(iota((2 * tiers, 2 * cols), 1), cols)
    picks = [
        jnp.where(
            ((sub8 == t) & (lane8 == 0)) | ((sub8 == tiers + t) & (lane8 == cols - 1)), 1.0, 0.0
        ).astype(BF16)
        for t in range(tiers)
    ]

    def halo_copy(turn, field, where, side, lands):
        if side < 2:
            src = field.at[0 if side == 0 else tiers - 1]
            dst = plane_recv.at[turn, lands]
        else:
            src = edge_send.at[turn, (side - 2) // 2]
            dst = edge_recv.at[turn, lands - 2]
        return pltpu.make_async_remote_copy(
            src_ref=src,
            dst_ref=dst,
            send_sem=halo_ssem.at[turn, side],
            recv_sem=halo_rsem.at[turn, lands],
            device_id=where,
            device_id_type=MESH,
        )

    def pack_rows(turn, field):
        for end in range(2):
            at = end * (rows - 1)
            for t in range(tiers):
                edge_send[turn, 0, end * tiers + t : end * tiers + t + 1, :] = field[t, at : at + 1, :]

    def pack_columns(turn, field):
        columns = jnp.zeros((2 * tiers, rows), F32)
        for t in range(tiers):
            columns = columns + lax.dot_general(
                picks[t], two_parts(field[t], 1), (((1,), (1,)), ((), ())), preferred_element_type=F32
            )
        edge_send[turn, 1] = columns

    def each_side(act, which=sides):
        for exists, where, side in which:
            pl.when(exists)(functools.partial(act, where, side))

    def start_halo(turn, field):
        def start(where, side):
            halo_copy(turn, field, where, side, side ^ 1).start()

        pack_rows(turn, field)
        each_side(start, sides[2:4])
        each_side(start, sides[:2])
        pack_columns(turn, field)
        each_side(start, sides[4:])

    def wait_halo(turn, field):
        each_side(lambda where, side: halo_copy(turn, field, where, side, side).wait_recv())

    def end_halo(turn, field):
        each_side(lambda where, side: halo_copy(turn, field, where, side, side ^ 1).wait_send())

    row_i = iota((rows, cols), 0)
    col_i = iota((rows, cols), 1)
    sub16 = mod(iota((8 * tiers, tiers * cols), 0), 4 * tiers)
    lane16 = iota((8 * tiers, tiers * cols), 1)
    put = jnp.where(
        ((mod(lane16, cols) == 0) & (sub16 == tiers + div(lane16, cols)))
        | ((mod(lane16, cols) == cols - 1) & (sub16 == 2 * tiers + div(lane16, cols))),
        1.0,
        0.0,
    ).astype(BF16)

    def inside(field, t):
        v = field[t]
        none = jnp.zeros_like(v)
        low = none if t == 0 else field[t - 1]
        high = none if t == tiers - 1 else field[t + 1]
        north = jnp.where(row_i == 0, 0.0, pltpu.roll(v, 1, 0))
        south = jnp.where(row_i == rows - 1, 0.0, pltpu.roll(v, rows - 1, 0))
        west = jnp.where(col_i == 0, 0.0, pltpu.roll(v, 1, 1))
        east = jnp.where(col_i == cols - 1, 0.0, pltpu.roll(v, cols - 1, 1))
        return v, (low, high, north, south, west, east)

    def rims(turn):
        ends = jnp.concatenate([edge_recv[turn, 2], edge_recv[turn, 3]], axis=0)
        return lax.dot_general(
            two_parts(ends, 0), put, (((0,), (0,)), ((), ())), preferred_element_type=F32
        )

    def apply_inside(field, t):
        v, around = inside(field, t)
        value = diag[t] * v
        for k in range(6):
            if not (k == 0 and t == 0 or k == 1 and t == tiers - 1):
                value = value - faces[k, t] * around[k]
        return value

    def add_beyond(turn):
        rim = rims(turn)
        resid[0] = resid[0] + faces[0, 0] * plane_recv[turn, 0]
        resid[tiers - 1] = resid[tiers - 1] + faces[1, tiers - 1] * plane_recv[turn, 1]
        for t in range(tiers):
            first, last = slice(0, 1), slice(rows - 1, rows)
            resid[t, first, :] = (
                resid[t, first, :] + faces[2, t, first, :] * edge_recv[turn, 0, tiers + t : tiers + t + 1, :]
            )
            resid[t, last, :] = (
                resid[t, last, :] + faces[3, t, last, :] * edge_recv[turn, 1, t : t + 1, :]
            )
            face = jnp.where(col_i == 0, faces[4, t], faces[5, t])
            resid[t] = resid[t] + face * rim[:, t * cols : (t + 1) * cols]

    beyond = (my_layer > 0).astype(jnp.int32) + (my_layer < n_layer - 1).astype(jnp.int32)
    pl.semaphore_wait(barrier, tiles - 1 + beyond)

    def note_copy(step):
        other, where = peer(step)
        return pltpu.make_async_remote_copy(
            src_ref=note_send.at[pl.ds(other * note_rows, note_rows), :],
            dst_ref=note_recv.at[pl.ds(me * note_rows, note_rows), :],
            send_sem=note_ssem.at[step],
            recv_sem=note_rsem.at[step],
            device_id=where,
            device_id_type=MESH,
        )

    half = wide // 2

    def load_copy(piece, other, lands):
        part = slice(piece * half, (piece + 1) * half)
        return pltpu.make_async_remote_copy(
            src_ref=load_send.at[pl.ds(other * PACK, PACK), part],
            dst_ref=load_recv.at[pl.ds(me * PACK, PACK), part],
            send_sem=load_ssem.at[piece, other],
            recv_sem=load_rsem.at[piece, lands],
            device_id={"row": div(other, n_col), "col": mod(other, n_col)},
            device_id_type=MESH,
        )

    own_load = pl.ds(pl.multiple_of(me * PACK, PACK), PACK)

    def own_move(piece):
        part = slice(piece * half, (piece + 1) * half)
        return pltpu.make_async_copy(
            load_send.at[own_load, part], load_recv.at[own_load, part], load_rsem.at[piece, me]
        )

    @pl.loop(1, tiles)
    def _(step):
        note_copy(step).start()

    own_note = pl.ds(pl.multiple_of(me * note_rows, note_rows), note_rows)
    own_copy = pltpu.make_async_copy(note_send.at[own_note, :], note_recv.at[own_note, :], note_rsem.at[0])
    own_copy.start()

    loads[6].wait()
    start_halo(0, temp)
    start_halo(1, cond)
    loads[7].wait()
    loads[8].wait()
    note_k = iota((slots, tiles * note_rows), 1)
    from_tile = jnp.where(
        (div(note_k, note_rows).astype(F32) == tgt_col) & (mod(note_k, note_rows) == 0), 1.0, 0.0
    )
    from_tile = jnp.concatenate([from_tile.astype(BF16)] * 3, axis=1)
    at_place = iota((slots, LANES), 1).astype(F32) == pos_col
    send_i = iota((tiles * PACK, folds * slots), 0)
    send_j = iota((tiles * PACK, folds * slots), 1)
    slot_place = jnp.concatenate([tgt_row * CAP + rank_row] * folds, axis=1)
    goes = (div(send_i, PACK) * CAP + mod(send_i, CAP)).astype(F32) == slot_place
    pick = jnp.where(goes & (div(mod(send_i, PACK), CAP) == div(send_j, slots)), 1.0, 0.0).astype(BF16)
    own_copy.wait()

    @pl.loop(1, tiles)
    def _(step):
        note_copy(step).wait_recv()

    head = note_recv[...].astype(BF16)
    rest = note_recv[...] - head.astype(F32)
    tile_means = jnp.dot(
        from_tile, jnp.concatenate([head, two_parts(rest, 0)], axis=0), preferred_element_type=F32
    )
    slot_mean = jnp.sum(jnp.where(at_place, tile_means, 0.0), axis=1, keepdims=True)
    block_rise = jnp.sum(same_block * to_row(slot_mean), axis=1, keepdims=True) / block_size
    factor = jnp.exp(sens_col * block_rise)
    for piece in range(2):
        slot_power = jnp.concatenate(
            [
                (
                    dyn[:, fold * wide + piece * half : fold * wide + (piece + 1) * half].astype(F32)
                    + factor
                    * leak[:, fold * wide + piece * half : fold * wide + (piece + 1) * half].astype(F32)
                ).astype(BF16)
                for fold in range(folds)
            ],
            axis=0,
        )
        load_send[:, piece * half : (piece + 1) * half] = jnp.dot(
            pick, slot_power, preferred_element_type=F32
        ).astype(BF16)

        @pl.loop(0, tiles)
        def _(step, piece=piece):
            nth = div(step, n_row)
            far = jnp.where(my_col < n_col // 2, n_col - 1 - nth, nth)
            other = lax.rem(my_row + lax.rem(step, n_row), n_row) * n_col + far

            @pl.when(other != me)
            def _():
                load_copy(piece, other, me).start()

        own_move(piece).start()

    loads[9].wait()
    wait_halo(0, temp)
    wait_halo(1, cond)
    rim = rims(1)
    for t in range(tiers):
        c, (low, high, north, south, west, east) = inside(cond, t)
        here = rim[:, t * cols : (t + 1) * cols]
        low = plane_recv[1, 0] if t == 0 else low
        high = plane_recv[1, 1] if t == tiers - 1 else high
        north = jnp.where(row_i == 0, edge_recv[1, 0, tiers + t : tiers + t + 1, :], north)
        south = jnp.where(row_i == rows - 1, edge_recv[1, 1, t : t + 1, :], south)
        west = jnp.where(col_i == 0, here, west)
        east = jnp.where(col_i == cols - 1, here, east)
        total = mass[t]
        for k, beside in enumerate((low, high, north, south, west, east)):
            face = 0.5 * (c + beside)
            faces[k, t] = face
            total = total + face
        diag[t] = total
        inv[t] = 1.0 / total
    for t in range(tiers):
        resid[t] = mass[t] * temp[t] - apply_inside(temp, t)
    add_beyond(0)

    middle = (EIG_LOW + EIG_HIGH) / 2.0
    spread = (EIG_HIGH - EIG_LOW) / 2.0
    ratio = middle / spread
    weight = 1.0 / ratio

    sel_i = iota((folds * patches, LANES), 0)
    sel_j = iota((folds * patches, LANES), 1)
    sel_in = mod(sel_i, patches)
    sel_patch = mod(sel_in, bands) * per_band + div(sel_in, bands)
    fold_hit = div(sel_i, patches) == div(mod(sel_j, PACK), CAP)
    notes = note_recv[...]
    pickers = []
    for chunk in range(chunks):
        code = jnp.sum(jnp.where(mod(note_j, note_rows) == 1 + chunk, notes, 0.0), axis=0, keepdims=True)
        pickers.append(
            jnp.where(fold_hit & (code == (sel_patch + 1).astype(F32)), 1.0, 0.0).astype(BF16)
        )

    picker = jnp.concatenate(pickers, axis=1)
    left = iota((bands, LANES), 1) < SUB
    for piece in range(2):
        own_move(piece).wait()

        @pl.loop(1, tiles)
        def _(step, piece=piece):
            other, _ = peer(step)
            load_copy(piece, other, other).wait_recv()

        footprint = jnp.dot(
            picker, load_recv[:, piece * half : (piece + 1) * half], preferred_element_type=F32
        )
        for fold in range(folds):
            for k in range(half // LANES):
                lanes = slice(k * LANES, (k + 1) * LANES)
                a = footprint[fold * patches : fold * patches + bands, lanes]
                b = footprint[fold * patches + bands : fold * patches + 2 * bands, lanes]
                at = 2 * (fold * (wide // LANES) + piece * (half // LANES) + k)
                power_ref[pl.ds(at, bands, stride=SUB), :] = jnp.where(left, a, pltpu.roll(b, SUB, 1))
                power_ref[pl.ds(at + 1, bands, stride=SUB), :] = jnp.where(
                    left, pltpu.roll(a, SUB, 1), b
                )

    def out_copy(t):
        return pltpu.make_async_copy(out_ref.at[t], out_hbm.at[t], out_sem.at[t])

    power_out = pltpu.make_async_copy(power_ref, power_hbm, out_sem.at[tiers])
    power_out.start()
    for t in range(tiers):
        r = resid[t] + power_ref[t * rows : (t + 1) * rows, :]
        resid[t] = r
        dirs[0, t] = r * inv[t] * (1.0 / middle)
    for sweep in range(1, SWEEPS):
        field = dirs.at[sweep - 1]
        turn = 1 + sweep
        start_halo(turn, field)
        weight_new = 1.0 / (2.0 * ratio - weight)
        for t in range(tiers):
            base = temp[t] if sweep == 1 else out_ref[t]
            out_ref[t] = base + field[t]
            resid[t] = resid[t] - apply_inside(field, t)
        wait_halo(turn, field)
        add_beyond(turn)
        for t in range(tiers):
            d = weight_new * weight * field[t] + (2.0 * weight_new / spread) * (resid[t] * inv[t])
            if sweep < SWEEPS - 1:
                dirs[sweep, t] = d
            else:
                out_ref[t] = out_ref[t] + d
                out_copy(t).start()
        weight = weight_new
    end_halo(0, temp)
    end_halo(1, cond)
    for sweep in range(1, SWEEPS):
        end_halo(1 + sweep, dirs.at[sweep - 1])

    @pl.loop(1, tiles)
    def _(step):
        note_copy(step).wait_send()
        other, _ = peer(step)
        load_copy(0, other, me).wait_send()
        load_copy(1, other, me).wait_send()

    power_out.wait()
    for t in range(tiers):
        out_copy(t).wait()


def hand_over(new, power, new_out, power_out, held, sem):
    planes = [(i, t) for i in range(2) for t in range(new.shape[0])]
    src, dst = (power, new), (power_out, new_out)
    takes = [pltpu.make_async_copy(src[i].at[t], held.at[i, t], sem.at[0, i, t]) for i, t in planes]
    gives = [pltpu.make_async_copy(held.at[i, t], dst[i].at[t], sem.at[1, i, t]) for i, t in planes]
    for take in takes:
        take.start()
    for take, give in zip(takes, gives):
        take.wait()
        give.start()
    for give in gives:
        give.wait()


def shards(sizes, temp, cond, mass, dyn, leak, panel, place, block, tier, sens):
    tiers, rows, cols = temp.shape
    slots, cells = dyn.shape[1:]
    tiles = sizes[0] * sizes[1]
    folds = PACK // CAP
    note_rows = -(-(1 + tiles * PACK // LANES) // 8) * 8
    any_spec = pl.BlockSpec(memory_space=pl.ANY)
    grid = (tiers, rows, cols)
    dma = pltpu.SemaphoreType.DMA
    new, power = pl.pallas_call(
        functools.partial(kernel, sizes),
        out_shape=(
            jax.ShapeDtypeStruct(grid, F32),
            jax.ShapeDtypeStruct((tiers * rows, cols), F32),
        ),
        in_specs=[any_spec] * 10,
        out_specs=(any_spec, any_spec),
        scratch_shapes=[
            pltpu.VMEM((1, slots), jnp.int32),
            pltpu.VMEM((1, slots), jnp.int32),
            pltpu.VMEM((1, slots), jnp.int32),
            pltpu.VMEM(tier.shape, jnp.int32),
            pltpu.VMEM(sens.shape, F32),
            pltpu.VMEM(grid, F32),
            pltpu.VMEM((tiers * rows, cols), F32),
            pltpu.VMEM(grid, F32),
            pltpu.VMEM(grid, F32),
            pltpu.VMEM(grid, F32),
            pltpu.VMEM((slots, cells), BF16),
            pltpu.VMEM((slots, cells), BF16),
            pltpu.VMEM((tiles * note_rows, LANES), F32),
            pltpu.VMEM((tiles * note_rows, LANES), F32),
            pltpu.VMEM((tiles * PACK, cells // folds), BF16),
            pltpu.VMEM((tiles * PACK, cells // folds), BF16),
            pltpu.VMEM((SWEEPS - 1,) + grid, F32),
            pltpu.VMEM((6,) + grid, F32),
            pltpu.VMEM(grid, F32),
            pltpu.VMEM(grid, F32),
            pltpu.VMEM(grid, F32),
            pltpu.VMEM((SWEEPS + 1, 2, 2 * tiers, cols), F32),
            pltpu.VMEM((SWEEPS + 1, 4, 2 * tiers, cols), F32),
            pltpu.VMEM((SWEEPS + 1, 2, rows, cols), F32),
            dma((10,)),
            dma((tiers + 1,)),
            dma((tiles,)),
            dma((tiles,)),
            dma((2, tiles)),
            dma((2, tiles)),
            dma((SWEEPS + 1, 6)),
            dma((SWEEPS + 1, 6)),
        ],
        compiler_params=pltpu.CompilerParams(
            collective_id=0, has_side_effects=True, vmem_limit_bytes=VMEM_BYTES
        ),
    )(temp, cond, mass, dyn, leak, panel.reshape(1, slots), place, block, tier, sens)
    return pl.pallas_call(
        hand_over,
        out_shape=(jax.ShapeDtypeStruct(grid, F32),) * 2,
        in_specs=[any_spec] * 2,
        out_specs=(any_spec, any_spec),
        scratch_shapes=[pltpu.VMEM((2,) + grid, F32), dma((2, 2, tiers))],
        compiler_params=pltpu.CompilerParams(vmem_limit_bytes=VMEM_BYTES),
    )(new, power.reshape(grid))


def solution(mesh):
    sizes = (mesh.shape["row"], mesh.shape["col"], mesh.shape["layer"])
    owner = ("row", "col", "layer")
    return jax.shard_map(
        functools.partial(shards, sizes),
        mesh=mesh,
        in_specs=(P("layer", "row", "col"),) * 3
        + (P(owner, None, None),) * 3
        + (P(owner, None),) * 4,
        out_specs=(P("layer", "row", "col"), P("layer", "row", "col")),
        check_vma=False,
    )
```
